256 devices in a mesh: dp: 128 (over y, z, x), rep: 2 (over core).
Axes of the slice: x: 4, y: 4, z: 8, core: 2. Of those that a mesh axis runs over, the one named last changes fastest.
Arguments:
- embeddings: float32 [131072, 1024], P(('dp', 'rep')), may hold values from -6 to 6
- cluster_ids: int32 [131072, 1], P(('dp', 'rep')), may hold values from 0 to 255; in each aligned block of 512 rows (0 to 511, 512 to 1023, ...) at most 4 rows name the same one
- boundary_slots: int32 [256, 2, 256], P(('dp', 'rep')), may hold values from 0 to 1023
Outputs:
- member_max: float32 [256, 1024], P(('dp', 'rep'))
- centrality: float32 [256, 1024], P(('dp', 'rep'))
The draws below stay inside these ranges and needn't reach their ends.
Inputs may be any that keep to these rules, and one draw needn't show every extreme that they name: `cluster_ids`: among the rows of one device, at most 4 name the same cluster, a bound that some block reaches of them; every cluster is named by some row.
All inputs are finite; a program needn't handle non-finite values.
Results may differ from the reference program's by a relative error of at most 0.0024.
Values may be sent and summed in bfloat16 or wider, within the bound.
A program may use at most 64 MiB of HBM per device.

```python
import math
import jax
import jax.numpy as jnp
import numpy as np
from jax import lax

E = 1024
SLOTS = 1024
BOUND = 256
CLUSTERS = 256
CAP = 4
ROWS_DEV = 512
ROWS = 131072


def set_ends(drawn, key, least, largest):
    index_at = [jax.random.randint(jax.random.fold_in(key, axis), (), 0, length) for axis, length in enumerate(drawn.shape)]
    main_axis = drawn.shape.index(max(drawn.shape))
    beside = index_at[:main_axis] + [(index_at[main_axis] + 1) % drawn.shape[main_axis]] + index_at[main_axis + 1:]
    return drawn.at[tuple(index_at)].set(least).at[tuple(beside)].set(largest)


def block_levels(rng, extent, split, least, high):
    level, own = 1.0, jax.random.fold_in(rng, 6)
    for dim, shards_of in split:
        steps = jnp.exp(jax.random.uniform(jax.random.fold_in(own, dim), (shards_of,), jnp.float32, least / len(split), high / len(split)))
        level = level * jnp.repeat(steps, extent[dim] // shards_of).reshape([-1 if axis == dim else 1 for axis in range(len(extent))])
    return level


def assign_block(rng, own, number, rows, count, top, most, lean):
    order = jax.random.permutation(rng, count)
    packed, common = portions_of(count, rows * top, most, lean, True), portions_of(count, rows * top, most, lean, False)
    places = jnp.arange(count)

    def named(lengths, turn):
        used = int((lengths > 0).sum())
        fixed = max(1, used // 4)
        shifted = fixed + (places - fixed + turn * (used - fixed)) % max(1, count - fixed)
        return jnp.zeros((count,), jnp.int32).at[order[jnp.where(places < fixed, places, shifted)]].set(jnp.asarray(lengths, jnp.int32))

    lengths = jnp.where(number % 4 == 0, named(packed, number // 4), named(common, number - number // 4 - 1))
    mixed = jax.random.permutation(jax.random.fold_in(own, 3), count)
    giver, taker = mixed[0:count // 2 * 2:2], mixed[1:count // 2 * 2:2]
    slack = jnp.minimum(lengths[giver] - 1, most - lengths[taker]) // 2
    slack = jnp.where((giver == order[0]) | (taker == order[0]) | (lengths[taker] == 0), 0, jnp.maximum(slack, 0))
    shifted = jax.random.randint(jax.random.fold_in(own, 4), (count // 2,), 0, 1 << 20) % (slack + 1)
    lengths = lengths.at[giver].add(-shifted).at[taker].add(shifted)
    items = jnp.searchsorted(jnp.cumsum(lengths), jnp.arange(rows * top), side="right").astype(jnp.int32)
    table = items.reshape(top, rows).T
    table = table[jax.random.permutation(jax.random.fold_in(own, 1), rows)]
    turn = jax.random.randint(jax.random.fold_in(own, 2), (rows, 1), 0, top)
    return jnp.take_along_axis(table, (jnp.arange(top)[None, :] + turn) % top, axis=1)


def portions_of(number_of, total, limit, slope, full):
    weights = [(1 << 20) // math.isqrt(grade ** slope) + 1 for grade in range(1, number_of + 1)]
    largest = limit if full else min(limit, max(-(-total // number_of), total * weights[0] // sum(weights)))
    least = 1 if total - largest >= number_of - 1 else 0
    given, spare = [largest] + [least] * (number_of - 1), total - largest - least * (number_of - 1)
    while spare > 0:
        movable = [i for i in range(1, number_of) if given[i] < largest] or [i for i in range(1, number_of) if given[i] < limit]
        pool, left = sum([weights[i] for i in movable]), spare
        for i in movable:
            addition = min(limit - given[i], max(1, left * weights[i] // pool), spare)
            given[i] = given[i] + addition
            spare = spare - addition
    return np.array(given)


def noise(rng, dims, scale, limit, split=(), held_as=jnp.bfloat16):
    drawn = scale * jax.random.normal(rng, dims, jnp.float32)
    if split:
        drawn = drawn * block_levels(rng, dims, split, -0.22, 0.18)
    return jnp.clip(drawn, -limit, limit).astype(held_as)


def setup_inputs(seed: int = 0) -> dict:
    splits = jax.random.split(jax.random.key(seed), 4)
    embeddings = noise(splits[0], (ROWS, E), 1.0, 6.0, ((0, 256),), jnp.float32)
    cluster_ids_keys = jax.random.split(jax.random.fold_in(splits[1], 1), ROWS // ROWS_DEV)
    cluster_ids_turns = jax.random.permutation(jax.random.fold_in(splits[1], 3), ROWS // ROWS_DEV)
    cluster_ids = jax.vmap(lambda own, number: assign_block(jax.random.fold_in(splits[1], 2), own, number, ROWS_DEV, CLUSTERS, 1, CAP, 2))(cluster_ids_keys, cluster_ids_turns).reshape((ROWS, 1))
    boundary_slots = set_ends(jax.random.randint(splits[2], (CLUSTERS, 2, BOUND), 0, SLOTS), jax.random.fold_in(splits[2], 1), 0, SLOTS - 1).astype(jnp.int32)
    return dict(embeddings=embeddings, cluster_ids=cluster_ids, boundary_slots=boundary_slots)


eps = 1e-06

def pick_rows(rows_table, positions):
    return rows_table[positions]

def reference(embeddings, cluster_ids, boundary_slots):
    capacity = SLOTS // CLUSTERS
    labels = cluster_ids[:, 0].astype(jnp.int32)
    unit_full = embeddings * lax.rsqrt(lax.optimization_barrier(jnp.sum(embeddings * embeddings, axis=1, keepdims=True)) + eps)
    unit_half = unit_full.astype(jnp.bfloat16)
    grouped = labels.reshape(CLUSTERS, ROWS_DEV)
    member_of = grouped[:, :, None] == jnp.arange(CLUSTERS, dtype=jnp.int32)[None, None, :]
    running = jnp.cumsum(member_of.astype(jnp.int32), axis=1)
    ranks = lax.optimization_barrier(jnp.sum(jnp.where(member_of, running, 0), axis=2)).astype(jnp.int32) - 1
    source = (jnp.arange(CLUSTERS * ROWS_DEV, dtype=jnp.int32) // ROWS_DEV).astype(jnp.int32)
    targets = (source * capacity + ranks.reshape(-1)).astype(jnp.int32)
    table = jnp.zeros((CLUSTERS, SLOTS, E), jnp.bfloat16).at[labels, targets].set(unit_half)
    filled = jnp.zeros((CLUSTERS, SLOTS), jnp.int32).at[labels, targets].set(1)
    sums = jax.ops.segment_sum(unit_half.astype(jnp.float32), labels, CLUSTERS)
    direction = sums * lax.rsqrt(lax.optimization_barrier(jnp.sum(sums * sums, axis=1, keepdims=True)) + eps)
    count = lax.optimization_barrier(jnp.sum(filled, axis=1)).astype(jnp.int32)
    order = jnp.argsort(1 - filled, axis=1, stable=True).astype(jnp.int32)
    picks = (boundary_slots % count[:, None, None]).astype(jnp.int32)
    positions = jnp.take_along_axis(order, picks.reshape(CLUSTERS, 2 * BOUND), axis=1)
    outward = jax.vmap(pick_rows)(table, positions)
    zeros_side = jnp.zeros((1, BOUND, E), jnp.bfloat16)
    lower_all = jnp.concatenate([zeros_side, outward[:-1, BOUND:]], axis=0)
    upper_all = jnp.concatenate([outward[1:, :BOUND], zeros_side], axis=0)

    def per_owner(items):
        members, usable, lower, upper, centre, owner = items
        valid = usable > 0
        candidates = jnp.concatenate([members, lower, upper], axis=0)
        scores = jnp.dot(members, candidates.T, preferred_element_type=jnp.float32)
        cand_ok = jnp.concatenate([valid, jnp.full((BOUND,), owner > 0), jnp.full((BOUND,), owner < CLUSTERS - 1)])
        column = jnp.arange(SLOTS + 2 * BOUND, dtype=jnp.int32)
        row_pos = jnp.arange(SLOTS, dtype=jnp.int32)
        keep = cand_ok[None, :] & (column[None, :] != row_pos[:, None])
        best = lax.optimization_barrier(jnp.max(jnp.where(keep, scores, -1.0), axis=1))
        nearest = jnp.where(valid, best, 0.0)
        central = jnp.dot(members.astype(jnp.float32), centre, precision=lax.Precision.HIGHEST)
        return (nearest, jnp.where(valid, central, 0.0))
    owners = jnp.arange(CLUSTERS, dtype=jnp.int32)
    member_max, centrality = lax.map(per_owner, (table, filled, lower_all, upper_all, direction, owners))
    return (member_max, centrality)
```

```python
import jax
import jax.numpy as jnp
from jax import lax
from jax.sharding import PartitionSpec as P

SLOTS = 1024


eps = 1e-06


def from_behind(array, axis, by):
    peers = lax.axis_size(axis)
    pairs = [(i, i + by) for i in range(peers) if 0 <= i + by < peers]
    return lax.ppermute(array, axis, pairs)


def per_device(embeddings, cluster_ids, boundary_slots):
    n_chips = lax.axis_size("dp")
    n_cores = lax.axis_size("rep")
    owners = n_chips * n_cores
    width = embeddings.shape[1]
    slots = SLOTS
    capacity = slots // owners
    bound = boundary_slots.shape[2]
    me = lax.axis_index(("dp", "rep"))
    labels = cluster_ids[:, 0]
    member_of = labels[:, None] == jnp.arange(owners, dtype=jnp.int32)[None, :]
    running = jnp.cumsum(member_of.astype(jnp.int32), axis=0)
    ranks = jnp.sum(jnp.where(member_of, running, 0), axis=1) - 1
    targets = labels * capacity + ranks
    unit_full = embeddings * lax.rsqrt(
        jnp.sum(embeddings * embeddings, axis=1, keepdims=True) + eps
    )
    unit_half = unit_full.astype(jnp.bfloat16)
    outgoing = jnp.zeros((slots, width), jnp.bfloat16).at[targets].set(unit_half)
    shaped = outgoing.reshape(n_chips, n_cores, capacity, width)
    arrived = lax.all_to_all(
        lax.all_to_all(shaped, "dp", split_axis=0, concat_axis=0, tiled=True),
        "rep",
        split_axis=1,
        concat_axis=1,
        tiled=True,
    )
    members = arrived.reshape(slots, width)
    own_sum = lax.dot_general(
        jnp.ones((1, slots), jnp.bfloat16), members, (((1,), (0,)), ((), ())), preferred_element_type=jnp.float32
    )
    direction = own_sum[0] * lax.rsqrt(jnp.sum(own_sum * own_sum) + eps)
    lengths = jnp.einsum("se,se->s", members, members, preferred_element_type=jnp.float32)
    filled = lengths > 0.5
    filled_int = filled.astype(jnp.int32)
    count = jnp.sum(filled_int)
    order = jnp.argsort(1 - filled_int, stable=True)
    picks = boundary_slots[0] % count
    positions = order[picks.reshape(-1)]
    outward = members[positions]
    lower = from_behind(outward[bound:], ("dp", "rep"), 1)
    upper = from_behind(outward[:bound], ("dp", "rep"), -1)
    candidates = jnp.concatenate([members, lower, upper], axis=0)
    cand_ok = jnp.concatenate(
        [filled, jnp.full((bound,), me > 0), jnp.full((bound,), me < owners - 1)]
    )
    column = jnp.arange(slots + 2 * bound, dtype=jnp.int32)
    block = min(512, slots)

    def one_block(start):
        block_rows = lax.dynamic_slice_in_dim(members, start, block, 0)
        scores = lax.dot_general(
            block_rows, candidates, (((1,), (1,)), ((), ())), preferred_element_type=jnp.float32
        )
        row_pos = start + jnp.arange(block, dtype=jnp.int32)
        keep = cand_ok[None, :] & (column[None, :] != row_pos[:, None])
        return jnp.max(jnp.where(keep, scores, -1.0), axis=1)

    starts = jnp.arange(slots // block, dtype=jnp.int32) * block
    best = lax.map(one_block, starts).reshape(slots)
    member_max = jnp.where(filled, best, 0.0)
    central = jnp.dot(
        members, direction, precision=lax.Precision.HIGHEST, preferred_element_type=jnp.float32
    )
    centrality = jnp.where(filled, central, 0.0)
    return (member_max[None, :], centrality[None, :])


def solution(mesh):
    placed = (P(("dp", "rep"), None), P(("dp", "rep"), None), P(("dp", "rep"), None, None))
    return jax.shard_map(
        per_device,
        mesh=mesh,
        in_specs=placed,
        out_specs=(P(("dp", "rep"), None), P(("dp", "rep"), None)),
        check_vma=False,
    )
```

```python
import functools

import jax
import jax.numpy as jnp
from jax import lax
from jax.experimental import pallas as pl
from jax.experimental.pallas import tpu as pltpu
from jax.sharding import PartitionSpec as P

MESH = pl.DeviceIdType.MESH
SLOTS = 1024
CAP = 4
Y, Z, X, C = 4, 8, 4, 2
DEVICES = Y * Z * X * C
SIDE = 16
EPS = 1e-06
MARK = 2.0
F32 = jnp.float32
BF16 = jnp.bfloat16


def iota(shape, dim):
    return lax.broadcasted_iota(jnp.int32, shape, dim)


def rows_dot(a, b):
    return lax.dot_general(a, b, (((1,), (1,)), ((), ())), preferred_element_type=F32)


def device(flat):
    return (flat // C, lax.rem(flat, C))


def kernel(
    emb_ref, lab_ref, bnd_ref, best_ref, cent_ref,
    out_buf, in_buf, members, picks, outward, lower, upper,
    stage_sem, send_sem, recv_sem, own_sem, side_send, side_recv,
):
    rows, width = emb_ref.shape
    bound = bnd_ref.shape[1]
    dp, core = lax.axis_index("dp"), lax.axis_index("rep")
    me = dp * C + core
    my_y, my_z, my_x = dp // (Z * X), lax.rem(dp // X, Z), lax.rem(dp, X)
    hi, lo = me // SIDE, lax.rem(me, SIDE)

    def row_mate(i):
        return hi * SIDE + lax.rem(lo + i, SIDE)

    def column_mate(i):
        return lax.rem(hi + i, SIDE) * SIDE + lo

    barrier = pltpu.get_barrier_semaphore()

    def greet(i, _):
        pl.semaphore_signal(barrier, inc=1, device_id=device(row_mate(i)), device_id_type=MESH)
        pl.semaphore_signal(barrier, inc=1, device_id=device(column_mate(i)), device_id_type=MESH)
        return 0

    lax.fori_loop(1, SIDE, greet, 0)

    lab = lab_ref[...].astype(F32)
    lab_col = jnp.broadcast_to(lab, (128, rows)).T
    lab_col = jnp.concatenate([lab_col] * (rows // 128), axis=1)
    earlier = (lab_col == lab) & (iota((rows, rows), 0) < iota((rows, rows), 1))
    rank = jnp.sum(jnp.where(earlier, 1.0, 0.0), axis=0, keepdims=True)
    target = lab * CAP + rank

    emb = emb_ref[...]
    unit = (emb * lax.rsqrt(jnp.sum(emb * emb, axis=1, keepdims=True) + EPS)).astype(BF16)

    pl.semaphore_wait(barrier, 2 * (SIDE - 1))

    def second(i, _):
        pl.semaphore_signal(stage_sem, inc=1, device_id=device(row_mate(i)), device_id_type=MESH)
        return 0

    lax.fori_loop(1, SIDE, second, 0)

    step = 128

    def build(i, _):
        slot = (iota((step, rows), 0) + i * step).astype(F32)
        chosen = slot == target
        some = jnp.sum(jnp.where(chosen, 1.0, 0.0), axis=1, keepdims=True)
        block = jnp.dot(jnp.where(chosen, 1.0, 0.0).astype(BF16), unit, preferred_element_type=F32)
        empty = (some < 0.5) & (iota((step, width), 1) == 0)
        block = jnp.where(empty, MARK, block)
        out_buf[pl.ds(i * (step // CAP), step // CAP)] = block.astype(BF16).reshape(step // CAP, CAP, width)
        return 0

    lax.fori_loop(0, SLOTS // step, build, 0)

    pl.semaphore_wait(stage_sem, SIDE - 1)

    plane = Y * X * C

    def send_to(dy, dz, dx, dc):
        t = (lax.rem(my_y + dy, Y) * Z + lax.rem(my_z + dz, Z)) * X + lax.rem(my_x + dx, X)
        c = lax.rem(core + dc, C)
        pltpu.make_async_remote_copy(
            out_buf.at[t * C + c], in_buf.at[me], send_sem, recv_sem.at[dz],
            device_id=(t, c), device_id_type=MESH,
        ).start()

    own = pltpu.make_async_copy(out_buf.at[me], in_buf.at[me], own_sem)
    own.start()
    for dz in (4, 3, 5, 2, 6, 1, 7, 0):
        def one(i, _, dz=dz):
            send_to(i // (X * C), dz, lax.rem(i // C, X), lax.rem(i, C))
            return 0

        lax.fori_loop(1 if dz == 0 else 0, plane, one, 0)

    raw = bnd_ref[...].astype(F32)
    for side in range(2):
        picks[pl.ds(side * bound, bound)] = jnp.broadcast_to(raw[side : side + 1], (128, bound)).T

    own.wait()
    for dz in (4, 3, 5, 2, 6, 1, 7, 0):
        n = plane - 1 if dz == 0 else plane
        pltpu.make_async_remote_copy(
            in_buf.at[pl.ds(0, n)], in_buf.at[pl.ds(0, n)], send_sem, recv_sem.at[dz],
            device_id=device(row_mate(1)), device_id_type=MESH,
        ).wait_recv()
        z = lax.rem(my_z + Z - dz, Z)
        for y in range(Y):
            first = y * (Z * X * C) + z * (X * C)
            members[pl.ds(pl.multiple_of(first * CAP, X * C * CAP), X * C * CAP)] = in_buf[
                pl.ds(first, X * C)
            ].reshape(X * C * CAP, width)

    corner = jnp.where(iota((8, 128), 1) == 0, 1.0, 0.0).astype(BF16)
    heads = rows_dot(corner, members[:, :128])[:1]
    filled = jnp.where(heads < 1.5, 1.0, 0.0)
    groups = SLOTS // 128
    stacked = jnp.concatenate([filled[:, k * 128 : (k + 1) * 128] for k in range(groups)], axis=0)
    upto = jnp.where(iota((128, 128), 0) <= iota((128, 128), 1), 1.0, 0.0).astype(BF16)
    within = jnp.dot(stacked.astype(BF16), upto, preferred_element_type=F32)
    totals = jnp.sum(stacked, axis=1, keepdims=True)
    count = jnp.sum(totals, axis=0, keepdims=True)
    order = []
    before = jnp.zeros((1, 1), F32)
    for k in range(groups):
        order.append(jnp.where(stacked[k : k + 1] > 0.5, within[k : k + 1] + (before - 1.0), -1.0))
        before = before + totals[k : k + 1]

    def choose(first, size):
        want = picks[pl.ds(first, size)]
        want = want - jnp.floor((want + 0.5) / count) * count
        return jnp.concatenate([jnp.where(want == order[k], 1.0, 0.0).astype(BF16) for k in range(groups)], axis=1)

    table = members[...]
    for side in range(2):
        outward[pl.ds(side * bound, bound)] = jnp.dot(
            choose(side * bound, bound), table, preferred_element_type=F32
        ).astype(BF16)
    above, below = lax.rem(me + 1, DEVICES), lax.rem(me + DEVICES - 1, DEVICES)
    up = pltpu.make_async_remote_copy(
        outward.at[pl.ds(bound, bound)], lower, side_send.at[0], side_recv.at[0],
        device_id=device(above), device_id_type=MESH,
    )
    down = pltpu.make_async_remote_copy(
        outward.at[pl.ds(0, bound)], upper, side_send.at[1], side_recv.at[1],
        device_id=device(below), device_id_type=MESH,
    )
    up.start()
    down.start()

    weights = jnp.broadcast_to(filled, (8, SLOTS)).astype(BF16)
    sums = jnp.dot(weights, table, preferred_element_type=F32)[:1]
    direction = sums * lax.rsqrt(jnp.sum(sums * sums, axis=1, keepdims=True) + EPS)
    high = direction.astype(BF16)
    rest = direction - high.astype(F32)
    middle = rest.astype(BF16)
    low = (rest - middle.astype(F32)).astype(BF16)
    row = iota((8, width), 0)
    parts = jnp.where(row == 0, high.astype(F32), jnp.where(row == 1, middle.astype(F32), jnp.where(row == 2, low.astype(F32), 0.0)))
    central = jnp.sum(rows_dot(parts.astype(BF16), table), axis=0, keepdims=True)
    cent_ref[...] = jnp.where(filled > 0.5, central, 0.0)

    chunk = 256
    best = jnp.full((8, SLOTS), -1.0, F32)
    for first in range(0, SLOTS, chunk):
        scores = rows_dot(members[first : first + chunk], table)
        empty = members[first : first + chunk, :128][:, :1].astype(F32) > 1.5
        barred = empty | (iota((chunk, SLOTS), 0) + first == iota((chunk, SLOTS), 1))
        scores = jnp.where(barred, -1.0, scores)
        best = jnp.maximum(best, jnp.max(scores.reshape(chunk // 8, 8, SLOTS), axis=0))

    up.wait()
    down.wait()
    for buf, there in ((lower, me > 0), (upper, me < DEVICES - 1)):
        scores = rows_dot(buf[...], table)
        top = jnp.max(scores.reshape(bound // 8, 8, SLOTS), axis=0)
        best = jnp.maximum(best, jnp.where(there, top, -1.0))
    nearest = jnp.max(best, axis=0, keepdims=True)
    best_ref[...] = jnp.where(filled > 0.5, nearest, 0.0)

    n = DEVICES - 1
    pltpu.make_async_remote_copy(
        out_buf.at[pl.ds(0, n)], out_buf.at[pl.ds(0, n)], send_sem, recv_sem.at[0],
        device_id=device(row_mate(1)), device_id_type=MESH,
    ).wait_send()


def per_device(embeddings, cluster_ids, boundary_slots):
    rows, width = embeddings.shape
    bound = boundary_slots.shape[2]
    vmem = pl.BlockSpec(memory_space=pltpu.VMEM)
    return pl.pallas_call(
        kernel,
        out_shape=(jax.ShapeDtypeStruct((1, SLOTS), F32), jax.ShapeDtypeStruct((1, SLOTS), F32)),
        in_specs=[vmem, vmem, vmem],
        out_specs=(vmem, vmem),
        scratch_shapes=[
            pltpu.VMEM((DEVICES, CAP, width), BF16),
            pltpu.VMEM((DEVICES, CAP, width), BF16),
            pltpu.VMEM((SLOTS, width), BF16),
            pltpu.VMEM((2 * bound, 128), F32),
            pltpu.VMEM((2 * bound, width), BF16),
            pltpu.VMEM((bound, width), BF16),
            pltpu.VMEM((bound, width), BF16),
            pltpu.SemaphoreType.REGULAR,
            pltpu.SemaphoreType.DMA,
            pltpu.SemaphoreType.DMA((Z,)),
            pltpu.SemaphoreType.DMA,
            pltpu.SemaphoreType.DMA((2,)),
            pltpu.SemaphoreType.DMA((2,)),
        ],
        compiler_params=pltpu.CompilerParams(collective_id=0, has_side_effects=True, vmem_limit_bytes=48 << 20),
    )(embeddings, cluster_ids.reshape(1, rows), boundary_slots[0])


def solution(mesh):
    placed = (P(("dp", "rep"), None), P(("dp", "rep"), None), P(("dp", "rep"), None, None))
    return jax.shard_map(
        per_device,
        mesh=mesh,
        in_specs=placed,
        out_specs=(P(("dp", "rep"), None), P(("dp", "rep"), None)),
        check_vma=False,
    )
```

```python
import functools

import jax
import jax.numpy as jnp
from jax import lax
from jax.experimental import pallas as pl
from jax.experimental.pallas import tpu as pltpu
from jax.sharding import PartitionSpec as P

MESH = pl.DeviceIdType.MESH
SLOTS = 1024
CAP = 4
DIRECT = 2
HOPPED = CAP - DIRECT
SPILL = 16
Y, Z, X, C = 4, 8, 4, 2
XC = X * C
PLANE = Y * XC
DEVICES = Z * PLANE
SIDE = 16
LANES = 128
EPS = 1e-06
EMPTY = 2.0
FULL = 8.0
ORDER = (4, 3, 5, 2, 6, 1, 7, 0)
F32 = jnp.float32
BF16 = jnp.bfloat16


def iota(shape, dim):
    return lax.broadcasted_iota(jnp.int32, shape, dim)


def rows_dot(a, b):
    return lax.dot_general(a, b, (((1,), (1,)), ((), ())), preferred_element_type=F32)


def device(flat):
    return (flat // C, lax.rem(flat, C))


def along_sublanes(row, size):
    turned = jnp.broadcast_to(row, (LANES, row.shape[1])).T
    return jnp.concatenate([turned] * (size // LANES), axis=1)


def earlier_equal(key, size):
    same = (along_sublanes(key, size) == key) & (iota((size, size), 0) < iota((size, size), 1))
    return jnp.sum(jnp.where(same, 1.0, 0.0), axis=0, keepdims=True)


def place():
    dp, core = lax.axis_index("dp"), lax.axis_index("rep")
    return dp * C + core, dp // (Z * X), lax.rem(dp // X, Z), lax.rem(dp, X), core


def row_mate(me, i):
    return me // SIDE * SIDE + lax.rem(me + i, SIDE)


def column_mate(me, i):
    return lax.rem(me // SIDE + i, SIDE) * SIDE + lax.rem(me, SIDE)


def greet(me):
    barrier = pltpu.get_barrier_semaphore()

    def one(i, _):
        pl.semaphore_signal(barrier, inc=1, device_id=device(row_mate(me, i)), device_id_type=MESH)
        pl.semaphore_signal(barrier, inc=1, device_id=device(column_mate(me, i)), device_id_type=MESH)
        return 0

    lax.fori_loop(1, SIDE, one, 0)


def pass_on(me, stage_sem):
    pl.semaphore_wait(pltpu.get_barrier_semaphore(), 2 * (SIDE - 1))

    def one(i, _):
        pl.semaphore_signal(stage_sem, inc=1, device_id=device(row_mate(me, i)), device_id_type=MESH)
        return 0

    lax.fori_loop(1, SIDE, one, 0)


def fetch(sources, targets, sems):
    copies = [pltpu.make_async_copy(s, t, sems.at[k]) for k, (s, t) in enumerate(zip(sources, targets))]
    for copy in copies:
        copy.start()
    return copies


def normalise(emb_ref, unit):
    rows = emb_ref.shape[0]
    step = 128

    def one(i, _):
        at = pl.ds(pl.multiple_of(i * step, step), step)
        emb = emb_ref[at, :]
        unit[at, :] = (emb * lax.rsqrt(jnp.sum(emb * emb, axis=1, keepdims=True) + EPS)).astype(BF16)
        return 0

    lax.fori_loop(0, rows // step, one, 0)


def build(target, unit, buf, total, per, full=None):
    rows, width = unit.shape
    step = 128

    def one(i, _):
        slot = (iota((step, rows), 0) + i * step).astype(F32)
        chosen = jnp.where(slot == target, 1.0, 0.0)
        some = jnp.sum(chosen, axis=1, keepdims=True)
        block = jnp.dot(chosen.astype(BF16), unit[...], preferred_element_type=F32)
        first = iota((step, width), 1) == 0
        block = jnp.where((some < 0.5) & first, EMPTY, block)
        if full is not None:
            block = jnp.where((full > 0.5) & first, FULL, block)
        buf[pl.ds(i * (step // per), step // per)] = block.astype(BF16).reshape(step // per, per, width)
        return 0

    lax.fori_loop(0, total // step, one, 0)


def turn_picks(bnd_ref, picks):
    bound = bnd_ref.shape[1]
    raw = bnd_ref[...].astype(F32)
    for side in range(2):
        picks[pl.ds(side * bound, bound)] = jnp.broadcast_to(raw[side : side + 1], (LANES, bound)).T


def send_group(place_of_me, dz, source, target, send_sem, recv_sem):
    me, my_y, my_z, my_x, core = place_of_me

    def one(i, _):
        t = (lax.rem(my_y + i // XC, Y) * Z + lax.rem(my_z + dz, Z)) * X + lax.rem(my_x + i // C, X)
        c = lax.rem(core + i, C)
        pltpu.make_async_remote_copy(
            source.at[t * C + c], target.at[me], send_sem, recv_sem.at[dz],
            device_id=(t, c), device_id_type=MESH,
        ).start()
        return 0

    lax.fori_loop(1 if dz == 0 else 0, PLANE, one, 0)


def awaited(me, ref, n, send_sem, recv_sem):
    view = ref.at[pl.ds(0, n)]
    return pltpu.make_async_remote_copy(
        view, view, send_sem, recv_sem, device_id=device(row_mate(me, 1)), device_id_type=MESH
    )


def finish(me, members, picks, outward, beside, side_send, side_recv, best_ref, cent_ref):
    width = members.shape[1]
    bound = outward.shape[0] // 2
    groups = SLOTS // LANES

    corner = jnp.where(iota((8, LANES), 1) == 0, 1.0, 0.0).astype(BF16)
    heads = rows_dot(corner, members[:, :LANES])[:1]
    filled = jnp.where(heads < 1.5, 1.0, 0.0)
    stacked = jnp.concatenate([filled[:, k * LANES : (k + 1) * LANES] for k in range(groups)], axis=0)
    upto = jnp.where(iota((LANES, LANES), 0) <= iota((LANES, LANES), 1), 1.0, 0.0).astype(BF16)
    within = jnp.dot(stacked.astype(BF16), upto, preferred_element_type=F32)
    totals = jnp.sum(stacked, axis=1, keepdims=True)
    count = jnp.sum(totals, axis=0, keepdims=True)
    order = []
    before = jnp.zeros((1, 1), F32)
    for k in range(groups):
        order.append(jnp.where(stacked[k : k + 1] > 0.5, within[k : k + 1] + (before - 1.0), -1.0))
        before = before + totals[k : k + 1]

    half = bound // 2
    above, below = lax.rem(me + 1, DEVICES), lax.rem(me + DEVICES - 1, DEVICES)
    table = members[...]
    copies = []
    for part in range(2):
        for side, peer in ((1, above), (0, below)):
            at = pl.ds(side * bound + part * half, half)
            want = picks[at]
            want = want - jnp.floor((want + 0.5) / count) * count
            chosen = [jnp.where(want == order[k], 1.0, 0.0).astype(BF16) for k in range(groups)]
            outward[at] = jnp.dot(jnp.concatenate(chosen, axis=1), table, preferred_element_type=F32).astype(BF16)
            copy = pltpu.make_async_remote_copy(
                outward.at[at], beside.at[at], side_send.at[side * 2 + part], side_recv.at[side * 2 + part],
                device_id=device(peer), device_id_type=MESH,
            )
            copy.start()
            copies.append((copy, side, at))

    weights = jnp.broadcast_to(filled, (8, SLOTS)).astype(BF16)
    sums = jnp.dot(weights, table, preferred_element_type=F32)[:1]
    direction = sums * lax.rsqrt(jnp.sum(sums * sums, axis=1, keepdims=True) + EPS)
    high = direction.astype(BF16)
    rest = direction - high.astype(F32)
    middle = rest.astype(BF16)
    low = (rest - middle.astype(F32)).astype(BF16)
    row = iota((8, width), 0)
    parts = jnp.where(row == 2, low.astype(F32), 0.0)
    parts = jnp.where(row == 1, middle.astype(F32), parts)
    parts = jnp.where(row == 0, high.astype(F32), parts)
    central = jnp.sum(rows_dot(parts.astype(BF16), table), axis=0, keepdims=True)
    cent_ref[...] = jnp.where(filled > 0.5, central, 0.0)

    chunk = 256
    best = jnp.full((8, SLOTS), -1.0, F32)
    for first in range(0, SLOTS, chunk):
        scores = rows_dot(members[first : first + chunk], table)
        empty = members[first : first + chunk, :LANES][:, :1].astype(F32) > 1.5
        barred = empty | (iota((chunk, SLOTS), 0) + first == iota((chunk, SLOTS), 1))
        scores = jnp.where(barred, -1.0, scores)
        best = jnp.maximum(best, jnp.max(scores.reshape(chunk // 8, 8, SLOTS), axis=0))
    for copy, side, at in copies:
        copy.wait()
        scores = rows_dot(beside[at], table)
        top = jnp.max(scores.reshape(half // 8, 8, SLOTS), axis=0)
        there = me > 0 if side == 1 else me < DEVICES - 1
        best = jnp.maximum(best, jnp.where(there, top, -1.0))
    nearest = jnp.max(best, axis=0, keepdims=True)
    best_ref[...] = jnp.where(filled > 0.5, nearest, 0.0)
    return heads


def ranked(lab_ref):
    labels = lab_ref[...]
    rows = labels.shape[1]
    return labels, earlier_equal(labels.astype(F32), rows)


def four_slot_kernel(
    emb_hbm, lab_hbm, bnd_hbm, best_ref, cent_ref,
    emb_ref, lab_ref, bnd_ref, unit, out_buf, in_buf, members, picks, outward, beside,
    in_sem, stage_sem, send_sem, recv_sem, own_sem, side_send, side_recv,
):
    width = emb_ref.shape[1]
    here = place()
    me, _, my_z, _, _ = here
    got = fetch((emb_hbm, lab_hbm, bnd_hbm), (emb_ref, lab_ref, bnd_ref), in_sem)
    greet(me)
    for copy in got:
        copy.wait()
    labels, rank = ranked(lab_ref)
    normalise(emb_ref, unit)
    pass_on(me, stage_sem)
    build(labels.astype(F32) * CAP + rank, unit, out_buf, SLOTS, CAP)
    pl.semaphore_wait(stage_sem, SIDE - 1)
    own = pltpu.make_async_copy(out_buf.at[me], in_buf.at[me], own_sem)
    own.start()
    for dz in ORDER:
        send_group(here, dz, out_buf, in_buf, send_sem, recv_sem)
    turn_picks(bnd_ref, picks)
    own.wait()
    for dz in ORDER:
        awaited(me, in_buf, PLANE - 1 if dz == 0 else PLANE, send_sem, recv_sem.at[dz]).wait_recv()
        z = lax.rem(my_z + Z - dz, Z)
        for y in range(Y):
            first = (y * Z + z) * XC
            members[pl.ds(pl.multiple_of(first * CAP, XC * CAP), XC * CAP)] = in_buf[pl.ds(first, XC)].reshape(
                XC * CAP, width
            )
    finish(me, members, picks, outward, beside, side_send, side_recv, best_ref, cent_ref)
    awaited(me, out_buf, DEVICES - 1, send_sem, recv_sem.at[0]).wait_send()


def two_hop_kernel(
    emb_hbm, lab_hbm, bnd_hbm, best_ref, cent_ref, full_ref,
    emb_ref, lab_ref, bnd_ref, unit, out_buf, in_buf, members, picks, outward, beside,
    out_spill, in_spill, out_code, in_code, out_hop, in_hop,
    in_sem, stage_sem, send_sem, recv_sem, own_sem, side_send, side_recv,
    spill_send, spill_recv, code_send, code_recv, hop_send, hop_recv,
):
    rows, width = emb_ref.shape
    here = place()
    me, my_y, my_z, my_x, core = here
    mine = (my_y * X + my_x) * C + core
    got = fetch((emb_hbm, lab_hbm, bnd_hbm), (emb_ref, lab_ref, bnd_ref), in_sem)
    greet(me)
    got[1].wait()
    labels, rank = ranked(lab_ref)
    spilled = rank > DIRECT - 0.5
    plane = (labels >> 3) & (Z - 1)
    within = ((labels >> 6) << 3) | (labels & (XC - 1))
    key = jnp.where(spilled, plane, Z).astype(F32)
    spot = earlier_equal(key, rows)
    fits = spilled & (spot < SPILL - 0.5)
    full = jnp.max(jnp.where(spilled & (spot > SPILL - 0.5), 1.0, 0.0), axis=1, keepdims=True)
    direct_at = jnp.where(spilled, -1.0, labels.astype(F32) * DIRECT + rank)
    spill_at = jnp.where(fits, plane.astype(F32) * SPILL + spot, -1.0)
    code = within.astype(F32) * HOPPED + rank + (1 - DIRECT)
    got[0].wait()
    normalise(emb_ref, unit)
    pass_on(me, stage_sem)

    lines = Z * SPILL
    chosen = jnp.where(iota((lines, rows), 0).astype(F32) == spill_at, 1.0, 0.0)
    out_spill[...] = (
        jnp.dot(chosen.astype(BF16), unit[...], preferred_element_type=F32).astype(BF16).reshape(Z, SPILL, width)
    )
    codes = jnp.sum(chosen * code, axis=1, keepdims=True)
    out_code[...] = jnp.broadcast_to(codes, (lines, LANES)).astype(BF16).reshape(Z, SPILL, LANES)
    build(direct_at, unit, out_buf, DEVICES * DIRECT, DIRECT, full)
    pl.semaphore_wait(stage_sem, SIDE - 1)

    def over(i, _):
        z = lax.rem(my_z + i, Z)
        to = ((my_y * Z + z) * X + my_x, core)
        pltpu.make_async_remote_copy(
            out_code.at[z], in_code.at[my_z], code_send, code_recv, device_id=to, device_id_type=MESH
        ).start()
        pltpu.make_async_remote_copy(
            out_spill.at[z], in_spill.at[my_z], spill_send, spill_recv, device_id=to, device_id_type=MESH
        ).start()
        return 0

    lax.fori_loop(1, Z, over, 0)
    own = fetch(
        (out_buf.at[me], out_spill.at[my_z], out_code.at[my_z]),
        (in_buf.at[me], in_spill.at[my_z], in_code.at[my_z]),
        own_sem,
    )
    early = 3
    for dz in ORDER[:early]:
        send_group(here, dz, out_buf, in_buf, send_sem, recv_sem)
    got[2].wait()
    turn_picks(bnd_ref, picks)
    for copy in own:
        copy.wait()

    awaited(me, in_code, Z - 1, code_send, code_recv).wait_recv()
    awaited(me, in_spill, Z - 1, spill_send, spill_recv).wait_recv()
    told = in_code[...].reshape(lines, LANES).astype(F32).T
    told = told[:1]
    owner = jnp.floor((told - 0.5) * (1.0 / HOPPED))
    line = owner * (Z * HOPPED) + (iota((1, lines), 1) >> 4).astype(F32) * HOPPED + (told - 1.0 - owner * HOPPED)
    line = jnp.where(told > 0.5, line, -1.0)
    came = in_spill[...].reshape(lines, width)
    step = 128
    for i in range(PLANE * Z * HOPPED // step):
        chosen = jnp.where((iota((step, lines), 0) + i * step).astype(F32) == line, 1.0, 0.0)
        some = jnp.sum(chosen, axis=1, keepdims=True)
        block = jnp.dot(chosen.astype(BF16), came, preferred_element_type=F32)
        block = jnp.where((some < 0.5) & (iota((step, width), 1) == 0), EMPTY, block)
        each = Z * HOPPED
        out_hop[pl.ds(i * (step // each), step // each)] = block.astype(BF16).reshape(step // each, Z, HOPPED, width)

    def around(i, _):
        y, x, c = lax.rem(my_y + i // XC, Y), lax.rem(my_x + i // C, X), lax.rem(core + i, C)
        pltpu.make_async_remote_copy(
            out_hop.at[(y * X + x) * C + c], in_hop.at[mine], hop_send, hop_recv,
            device_id=((y * Z + my_z) * X + x, c), device_id_type=MESH,
        ).start()
        return 0

    lax.fori_loop(1, PLANE, around, 0)
    kept = pltpu.make_async_copy(out_hop.at[mine], in_hop.at[mine], own_sem.at[0])
    kept.start()
    for dz in ORDER[early:]:
        send_group(here, dz, out_buf, in_buf, send_sem, recv_sem)
    kept.wait()
    awaited(me, in_hop, PLANE - 1, hop_send, hop_recv).wait_recv()

    lines = PLANE * CAP
    a, b = iota((lines, lines), 0), iota((lines, lines), 1)
    k = a & (CAP - 1)
    source = (a >> 2) * DIRECT + (k & (DIRECT - 1)) + jnp.where(k >= DIRECT, PLANE * DIRECT, 0)
    mixing = jnp.where(source == b, 1.0, 0.0).astype(BF16)
    for dz in ORDER:
        awaited(me, in_buf, PLANE - 1 if dz == 0 else PLANE, send_sem, recv_sem.at[dz]).wait_recv()
        z = lax.rem(my_z + Z - dz, Z)
        blocks = [in_buf[pl.ds((y * Z + z) * XC, XC)].reshape(XC * DIRECT, width) for y in range(Y)]
        blocks.append(in_hop[:, z].reshape(PLANE * HOPPED, width))
        mixed = jnp.dot(mixing, jnp.concatenate(blocks, axis=0), preferred_element_type=F32).astype(BF16)
        for y in range(Y):
            first = (y * Z + z) * XC * CAP
            members[pl.ds(pl.multiple_of(first, XC * CAP), XC * CAP)] = mixed[y * XC * CAP : (y + 1) * XC * CAP]
    heads = finish(me, members, picks, outward, beside, side_send, side_recv, best_ref, cent_ref)
    full_ref[...] = jnp.broadcast_to(jnp.max(heads, axis=1, keepdims=True), full_ref.shape)

    awaited(me, out_buf, DEVICES - 1, send_sem, recv_sem.at[0]).wait_send()
    awaited(me, out_spill, Z - 1, spill_send, spill_recv).wait_send()
    awaited(me, out_code, Z - 1, code_send, code_recv).wait_send()
    awaited(me, out_hop, PLANE - 1, hop_send, hop_recv).wait_send()


def per_device(embeddings, cluster_ids, boundary_slots):
    rows, width = embeddings.shape
    bound = boundary_slots.shape[2]
    labels, ranks = cluster_ids.reshape(1, rows), boundary_slots[0]
    line = jax.ShapeDtypeStruct((1, SLOTS), F32)
    vmem, anywhere = pl.BlockSpec(memory_space=pltpu.VMEM), pl.BlockSpec(memory_space=pl.ANY)
    dma = pltpu.SemaphoreType.DMA

    def buffers(per):
        return [
            pltpu.VMEM((rows, width), F32),
            pltpu.VMEM((1, rows), jnp.int32),
            pltpu.VMEM((2, bound), jnp.int32),
            pltpu.VMEM((rows, width), BF16),
            pltpu.VMEM((DEVICES, per, width), BF16),
            pltpu.VMEM((DEVICES, per, width), BF16),
            pltpu.VMEM((SLOTS, width), BF16),
            pltpu.VMEM((2 * bound, LANES), F32),
            pltpu.VMEM((2 * bound, width), BF16),
            pltpu.VMEM((2 * bound, width), BF16),
        ]

    sems = [dma((3,)), pltpu.SemaphoreType.REGULAR, dma, dma((Z,))]

    def call(body, outs, scratch, number):
        return pl.pallas_call(
            body,
            out_shape=outs,
            in_specs=[anywhere] * 3,
            out_specs=(vmem,) * len(outs),
            scratch_shapes=scratch,
            compiler_params=pltpu.CompilerParams(
                collective_id=number, has_side_effects=True, vmem_limit_bytes=48 << 20
            ),
        )(embeddings, labels, ranks)

    best, central, full = call(
        two_hop_kernel,
        (line, line, jax.ShapeDtypeStruct((1, LANES), F32)),
        buffers(DIRECT)
        + [
            pltpu.VMEM((Z, SPILL, width), BF16),
            pltpu.VMEM((Z, SPILL, width), BF16),
            pltpu.VMEM((Z, SPILL, LANES), BF16),
            pltpu.VMEM((Z, SPILL, LANES), BF16),
            pltpu.VMEM((PLANE, Z, HOPPED, width), BF16),
            pltpu.VMEM((PLANE, Z, HOPPED, width), BF16),
        ]
        + sems
        + [dma((3,)), dma((4,)), dma((4,))]
        + [dma] * 6,
        0,
    )

    def again():
        return tuple(call(four_slot_kernel, (line, line), buffers(CAP) + sems + [dma, dma((4,)), dma((4,))], 1))

    return lax.cond(full[0, 0] > 4.0, again, lambda: (best, central))


def solution(mesh):
    placed = (P(("dp", "rep"), None), P(("dp", "rep"), None), P(("dp", "rep"), None, None))
    return jax.shard_map(
        per_device,
        mesh=mesh,
        in_specs=placed,
        out_specs=(P(("dp", "rep"), None), P(("dp", "rep"), None)),
        check_vma=False,
    )
```

```python
import functools

import jax
import jax.numpy as jnp
from jax import lax
from jax.experimental import pallas as pl
from jax.experimental.pallas import tpu as pltpu
from jax.sharding import PartitionSpec as P

MESH = pl.DeviceIdType.MESH
SLOTS = 1024
CAP = 4
DIRECT = 2
HOPPED = CAP - DIRECT
SPILL = 16
Y, Z, X, C = 4, 8, 4, 2
XC = X * C
PLANE = Y * XC
DEVICES = Z * PLANE
SIDE = 16
LANES = 128
EPS = 1e-06
EMPTY = 2.0
FULL = 8.0
ORDER = (0, 1, 7, 2, 6, 4, 3, 5)
F32 = jnp.float32
BF16 = jnp.bfloat16


def iota(shape, dim):
    return lax.broadcasted_iota(jnp.int32, shape, dim)


def rows_dot(a, b):
    return lax.dot_general(a, b, (((1,), (1,)), ((), ())), preferred_element_type=F32)


def device(flat):
    return (flat // C, lax.rem(flat, C))


def along_sublanes(row, size):
    turned = jnp.broadcast_to(row, (LANES, row.shape[1])).T
    return jnp.concatenate([turned] * (size // LANES), axis=1)


def earlier_equal(key, size):
    same = (along_sublanes(key, size) == key) & (iota((size, size), 0) < iota((size, size), 1))
    return jnp.sum(jnp.where(same, 1.0, 0.0), axis=0, keepdims=True)


def place():
    dp, core = lax.axis_index("dp"), lax.axis_index("rep")
    return dp * C + core, dp // (Z * X), lax.rem(dp // X, Z), lax.rem(dp, X), core


def row_mate(me, i):
    y, z, x, c = me // (Z * XC), lax.rem(me // XC, Z), lax.rem(me // C, X), lax.rem(me, C)
    return ((y * Z + lax.rem(z + i // C, Z)) * X + x) * C + lax.rem(c + i, C)


def column_mate(me, i):
    y, z, x, c = me // (Z * XC), lax.rem(me // XC, Z), lax.rem(me // C, X), lax.rem(me, C)
    return ((lax.rem(y + i // X, Y) * Z + z) * X + lax.rem(x + i, X)) * C + c


def greet(me):
    barrier = pltpu.get_barrier_semaphore()

    def one(i, _):
        pl.semaphore_signal(barrier, inc=1, device_id=device(row_mate(me, i)), device_id_type=MESH)
        pl.semaphore_signal(barrier, inc=1, device_id=device(column_mate(me, i)), device_id_type=MESH)
        return 0

    lax.fori_loop(1, SIDE, one, 0)


def pass_on(me, stage_sem):
    pl.semaphore_wait(pltpu.get_barrier_semaphore(), 2 * (SIDE - 1))

    def one(i, _):
        pl.semaphore_signal(stage_sem, inc=1, device_id=device(row_mate(me, i)), device_id_type=MESH)
        return 0

    lax.fori_loop(1, SIDE, one, 0)


def fetch(sources, targets, sems):
    copies = [pltpu.make_async_copy(s, t, sems.at[k]) for k, (s, t) in enumerate(zip(sources, targets))]
    for copy in copies:
        copy.start()
    return copies


def normalise(emb_ref, unit):
    rows = emb_ref.shape[0]
    step = 128

    def one(i, _):
        at = pl.ds(pl.multiple_of(i * step, step), step)
        emb = emb_ref[at, :]
        unit[at, :] = (emb * lax.rsqrt(jnp.sum(emb * emb, axis=1, keepdims=True) + EPS)).astype(BF16)
        return 0

    lax.fori_loop(0, rows // step, one, 0)


def build(target, unit, buf, total, per, full=None):
    rows, width = unit.shape
    step = 128

    def one(i, _):
        slot = (iota((step, rows), 0) + i * step).astype(F32)
        chosen = jnp.where(slot == target, 1.0, 0.0)
        some = jnp.sum(chosen, axis=1, keepdims=True)
        block = jnp.dot(chosen.astype(BF16), unit[...], preferred_element_type=F32)
        first = iota((step, width), 1) == 0
        block = jnp.where((some < 0.5) & first, EMPTY, block)
        if full is not None:
            block = jnp.where((full > 0.5) & first, FULL, block)
        buf[pl.ds(i * (step // per), step // per)] = block.astype(BF16).reshape(step // per, per, width)
        return 0

    lax.fori_loop(0, total // step, one, 0)


def turn_picks(bnd_ref, picks):
    bound = bnd_ref.shape[1]
    raw = bnd_ref[...].astype(F32)
    for side in range(2):
        picks[pl.ds(side * bound, bound)] = jnp.broadcast_to(raw[side : side + 1], (LANES, bound)).T


def in_plane(place_of_me, i):
    _, my_y, _, my_x, core = place_of_me
    return lax.rem(my_y + i // XC, Y), lax.rem(my_x + i // C, X), lax.rem(core + i, C)


def send_one(place_of_me, dz, i, source, target, send_sem, recv_sem):
    y, x, c = in_plane(place_of_me, i)
    t = (y * Z + lax.rem(place_of_me[2] + dz, Z)) * X + x
    pltpu.make_async_remote_copy(
        source.at[t * C + c], target.at[place_of_me[0]], send_sem, recv_sem.at[dz],
        device_id=(t, c), device_id_type=MESH,
    ).start()


def send_group(place_of_me, dzs, source, target, send_sem, recv_sem, beside=None):
    def one(i, _):
        if beside is not None:
            beside(i)
        for dz in dzs:
            send_one(place_of_me, dz, i, source, target, send_sem, recv_sem)
        return 0

    for dz in dzs:
        if dz:
            send_one(place_of_me, dz, 0, source, target, send_sem, recv_sem)
    lax.fori_loop(1, PLANE, one, 0)


def awaited(me, ref, n, send_sem, recv_sem):
    view = ref.at[pl.ds(0, n)]
    return pltpu.make_async_remote_copy(
        view, view, send_sem, recv_sem, device_id=device(row_mate(me, 1)), device_id_type=MESH
    )


def finish(me, members, picks, outward, beside, side_send, side_recv, best_ref, cent_ref):
    width = members.shape[1]
    bound = outward.shape[0] // 2
    groups = SLOTS // LANES

    corner = jnp.where(iota((8, LANES), 1) == 0, 1.0, 0.0).astype(BF16)
    heads = rows_dot(corner, members[:, :LANES])[:1]
    filled = jnp.where(heads < 1.5, 1.0, 0.0)
    stacked = jnp.concatenate([filled[:, k * LANES : (k + 1) * LANES] for k in range(groups)], axis=0)
    upto = jnp.where(iota((LANES, LANES), 0) <= iota((LANES, LANES), 1), 1.0, 0.0).astype(BF16)
    within = jnp.dot(stacked.astype(BF16), upto, preferred_element_type=F32)
    totals = jnp.sum(stacked, axis=1, keepdims=True)
    count = jnp.sum(totals, axis=0, keepdims=True)
    order = []
    before = jnp.zeros((1, 1), F32)
    for k in range(groups):
        order.append(jnp.where(stacked[k : k + 1] > 0.5, within[k : k + 1] + (before - 1.0), -1.0))
        before = before + totals[k : k + 1]

    half = bound // 2
    above, below = lax.rem(me + 1, DEVICES), lax.rem(me + DEVICES - 1, DEVICES)
    table = members[...]
    copies = []
    for part in range(2):
        for side, peer in ((1, above), (0, below)):
            at = pl.ds(side * bound + part * half, half)
            want = picks[at]
            want = want - jnp.floor((want + 0.5) / count) * count
            chosen = [jnp.where(want == order[k], 1.0, 0.0).astype(BF16) for k in range(groups)]
            outward[at] = jnp.dot(jnp.concatenate(chosen, axis=1), table, preferred_element_type=F32).astype(BF16)
            copy = pltpu.make_async_remote_copy(
                outward.at[at], beside.at[at], side_send.at[side * 2 + part], side_recv.at[side * 2 + part],
                device_id=device(peer), device_id_type=MESH,
            )
            copy.start()
            copies.append((copy, side, at))

    weights = jnp.broadcast_to(filled, (8, SLOTS)).astype(BF16)
    sums = jnp.dot(weights, table, preferred_element_type=F32)[:1]
    direction = sums * lax.rsqrt(jnp.sum(sums * sums, axis=1, keepdims=True) + EPS)
    high = direction.astype(BF16)
    rest = direction - high.astype(F32)
    middle = rest.astype(BF16)
    low = (rest - middle.astype(F32)).astype(BF16)
    row = iota((8, width), 0)
    parts = jnp.where(row == 2, low.astype(F32), 0.0)
    parts = jnp.where(row == 1, middle.astype(F32), parts)
    parts = jnp.where(row == 0, high.astype(F32), parts)
    central = jnp.sum(rows_dot(parts.astype(BF16), table), axis=0, keepdims=True)
    cent_ref[...] = jnp.where(filled > 0.5, central, 0.0)

    chunk = 256
    best = jnp.full((8, SLOTS), -1.0, F32)
    for first in range(0, SLOTS, chunk):
        scores = rows_dot(members[first : first + chunk], table)
        empty = members[first : first + chunk, :LANES][:, :1].astype(F32) > 1.5
        barred = empty | (iota((chunk, SLOTS), 0) + first == iota((chunk, SLOTS), 1))
        scores = jnp.where(barred, -1.0, scores)
        best = jnp.maximum(best, jnp.max(scores.reshape(chunk // 8, 8, SLOTS), axis=0))
    for copy, side, at in copies:
        copy.wait()
        scores = rows_dot(beside[at], table)
        top = jnp.max(scores.reshape(half // 8, 8, SLOTS), axis=0)
        there = me > 0 if side == 1 else me < DEVICES - 1
        best = jnp.maximum(best, jnp.where(there, top, -1.0))
    nearest = jnp.max(best, axis=0, keepdims=True)
    best_ref[...] = jnp.where(filled > 0.5, nearest, 0.0)
    return heads


def ranked(lab_ref):
    labels = lab_ref[...]
    rows = labels.shape[1]
    return labels, earlier_equal(labels.astype(F32), rows)


def four_slot_kernel(
    emb_hbm, lab_hbm, bnd_hbm, best_ref, cent_ref,
    emb_ref, lab_ref, bnd_ref, unit, out_buf, in_buf, members, picks, outward, beside,
    in_sem, stage_sem, send_sem, recv_sem, own_sem, side_send, side_recv,
):
    width = emb_ref.shape[1]
    here = place()
    me, _, my_z, _, _ = here
    got = fetch((emb_hbm, lab_hbm, bnd_hbm), (emb_ref, lab_ref, bnd_ref), in_sem)
    greet(me)
    for copy in got:
        copy.wait()
    labels, rank = ranked(lab_ref)
    normalise(emb_ref, unit)
    pass_on(me, stage_sem)
    build(labels.astype(F32) * CAP + rank, unit, out_buf, SLOTS, CAP)
    pl.semaphore_wait(stage_sem, SIDE - 1)
    own = pltpu.make_async_copy(out_buf.at[me], in_buf.at[me], own_sem)
    own.start()
    for dz in ORDER:
        send_group(here, (dz,), out_buf, in_buf, send_sem, recv_sem)
    turn_picks(bnd_ref, picks)
    own.wait()
    for dz in ORDER:
        awaited(me, in_buf, PLANE - 1 if dz == 0 else PLANE, send_sem, recv_sem.at[dz]).wait_recv()
        z = lax.rem(my_z + Z - dz, Z)
        for y in range(Y):
            first = (y * Z + z) * XC
            members[pl.ds(pl.multiple_of(first * CAP, XC * CAP), XC * CAP)] = in_buf[pl.ds(first, XC)].reshape(
                XC * CAP, width
            )
    finish(me, members, picks, outward, beside, side_send, side_recv, best_ref, cent_ref)
    awaited(me, out_buf, DEVICES - 1, send_sem, recv_sem.at[0]).wait_send()


def two_hop_kernel(
    emb_hbm, lab_hbm, bnd_hbm, best_ref, cent_ref, full_ref,
    emb_ref, lab_ref, bnd_ref, unit, out_buf, in_buf, members, picks, outward, beside,
    out_spill, in_spill, out_code, in_code, out_hop, in_hop,
    in_sem, stage_sem, send_sem, recv_sem, own_sem, side_send, side_recv,
    spill_send, spill_recv, code_send, code_recv, hop_send, hop_recv,
):
    rows, width = emb_ref.shape
    here = place()
    me, my_y, my_z, my_x, core = here
    mine = (my_y * X + my_x) * C + core
    got = fetch((emb_hbm, lab_hbm, bnd_hbm), (emb_ref, lab_ref, bnd_ref), in_sem)
    greet(me)
    got[1].wait()
    labels, rank = ranked(lab_ref)
    spilled = rank > DIRECT - 0.5
    plane = (labels >> 3) & (Z - 1)
    within = ((labels >> 6) << 3) | (labels & (XC - 1))
    key = jnp.where(spilled, plane, Z).astype(F32)
    spot = earlier_equal(key, rows)
    fits = spilled & (spot < SPILL - 0.5)
    full = jnp.max(jnp.where(spilled & (spot > SPILL - 0.5), 1.0, 0.0), axis=1, keepdims=True)
    direct_at = jnp.where(spilled, -1.0, labels.astype(F32) * DIRECT + rank)
    spill_at = jnp.where(fits, plane.astype(F32) * SPILL + spot, -1.0)
    code = within.astype(F32) * HOPPED + rank + (1 - DIRECT)
    pass_on(me, stage_sem)
    got[0].wait()
    normalise(emb_ref, unit)

    lines = Z * SPILL
    chosen = jnp.where(iota((lines, rows), 0).astype(F32) == spill_at, 1.0, 0.0)
    out_spill[...] = (
        jnp.dot(chosen.astype(BF16), unit[...], preferred_element_type=F32).astype(BF16).reshape(Z, SPILL, width)
    )
    codes = jnp.sum(chosen * code, axis=1, keepdims=True)
    out_code[...] = jnp.broadcast_to(codes, (lines, LANES)).astype(BF16).reshape(Z, SPILL, LANES)

    def over(i, _):
        z = lax.rem(my_z + i, Z)
        to = ((my_y * Z + z) * X + my_x, core)
        pltpu.make_async_remote_copy(
            out_code.at[z], in_code.at[my_z], code_send, code_recv, device_id=to, device_id_type=MESH
        ).start()
        pltpu.make_async_remote_copy(
            out_spill.at[z], in_spill.at[my_z], spill_send, spill_recv, device_id=to, device_id_type=MESH
        ).start()
        return 0

    lax.fori_loop(1, Z, over, 0)
    build(direct_at, unit, out_buf, DEVICES * DIRECT, DIRECT, full)
    pl.semaphore_wait(stage_sem, SIDE - 1)
    own = fetch(
        (out_buf.at[me], out_spill.at[my_z], out_code.at[my_z]),
        (in_buf.at[me], in_spill.at[my_z], in_code.at[my_z]),
        own_sem,
    )
    early = 5
    send_group(here, ORDER[:early], out_buf, in_buf, send_sem, recv_sem)
    got[2].wait()
    turn_picks(bnd_ref, picks)
    for copy in own:
        copy.wait()

    awaited(me, in_code, Z - 1, code_send, code_recv).wait_recv()
    awaited(me, in_spill, Z - 1, spill_send, spill_recv).wait_recv()
    told = in_code[...].reshape(lines, LANES).astype(F32).T
    told = told[:1]
    owner = jnp.floor((told - 0.5) * (1.0 / HOPPED))
    line = owner * (Z * HOPPED) + (iota((1, lines), 1) >> 4).astype(F32) * HOPPED + (told - 1.0 - owner * HOPPED)
    line = jnp.where(told > 0.5, line, -1.0)
    came = in_spill[...].reshape(lines, width)
    step = 128
    for i in range(PLANE * Z * HOPPED // step):
        chosen = jnp.where((iota((step, lines), 0) + i * step).astype(F32) == line, 1.0, 0.0)
        some = jnp.sum(chosen, axis=1, keepdims=True)
        block = jnp.dot(chosen.astype(BF16), came, preferred_element_type=F32)
        block = jnp.where((some < 0.5) & (iota((step, width), 1) == 0), EMPTY, block)
        each = Z * HOPPED
        out_hop[pl.ds(i * (step // each), step // each)] = block.astype(BF16).reshape(step // each, Z, HOPPED, width)

    def around(i):
        y, x, c = in_plane(here, i)
        pltpu.make_async_remote_copy(
            out_hop.at[(y * X + x) * C + c], in_hop.at[mine], hop_send, hop_recv,
            device_id=((y * Z + my_z) * X + x, c), device_id_type=MESH,
        ).start()

    kept = pltpu.make_async_copy(out_hop.at[mine], in_hop.at[mine], own_sem.at[0])
    kept.start()
    send_group(here, ORDER[early:], out_buf, in_buf, send_sem, recv_sem, around)
    kept.wait()
    awaited(me, in_hop, PLANE - 1, hop_send, hop_recv).wait_recv()

    lines = PLANE * CAP
    a, b = iota((lines, lines), 0), iota((lines, lines), 1)
    k = a & (CAP - 1)
    source = (a >> 2) * DIRECT + (k & (DIRECT - 1)) + jnp.where(k >= DIRECT, PLANE * DIRECT, 0)
    mixing = jnp.where(source == b, 1.0, 0.0).astype(BF16)
    for dz in ORDER:
        awaited(me, in_buf, PLANE - 1 if dz == 0 else PLANE, send_sem, recv_sem.at[dz]).wait_recv()
        z = lax.rem(my_z + Z - dz, Z)
        blocks = [in_buf[pl.ds((y * Z + z) * XC, XC)].reshape(XC * DIRECT, width) for y in range(Y)]
        blocks.append(in_hop[:, z].reshape(PLANE * HOPPED, width))
        mixed = jnp.dot(mixing, jnp.concatenate(blocks, axis=0), preferred_element_type=F32).astype(BF16)
        for y in range(Y):
            first = (y * Z + z) * XC * CAP
            members[pl.ds(pl.multiple_of(first, XC * CAP), XC * CAP)] = mixed[y * XC * CAP : (y + 1) * XC * CAP]
    heads = finish(me, members, picks, outward, beside, side_send, side_recv, best_ref, cent_ref)
    full_ref[...] = jnp.broadcast_to(jnp.max(heads, axis=1, keepdims=True), full_ref.shape)

    awaited(me, out_buf, DEVICES - 1, send_sem, recv_sem.at[0]).wait_send()
    awaited(me, out_spill, Z - 1, spill_send, spill_recv).wait_send()
    awaited(me, out_code, Z - 1, code_send, code_recv).wait_send()
    awaited(me, out_hop, PLANE - 1, hop_send, hop_recv).wait_send()


def per_device(embeddings, cluster_ids, boundary_slots):
    rows, width = embeddings.shape
    bound = boundary_slots.shape[2]
    labels, ranks = cluster_ids.reshape(1, rows), boundary_slots[0]
    line = jax.ShapeDtypeStruct((1, SLOTS), F32)
    vmem, anywhere = pl.BlockSpec(memory_space=pltpu.VMEM), pl.BlockSpec(memory_space=pl.ANY)
    dma = pltpu.SemaphoreType.DMA

    def buffers(per):
        return [
            pltpu.VMEM((rows, width), F32),
            pltpu.VMEM((1, rows), jnp.int32),
            pltpu.VMEM((2, bound), jnp.int32),
            pltpu.VMEM((rows, width), BF16),
            pltpu.VMEM((DEVICES, per, width), BF16),
            pltpu.VMEM((DEVICES, per, width), BF16),
            pltpu.VMEM((SLOTS, width), BF16),
            pltpu.VMEM((2 * bound, LANES), F32),
            pltpu.VMEM((2 * bound, width), BF16),
            pltpu.VMEM((2 * bound, width), BF16),
        ]

    sems = [dma((3,)), pltpu.SemaphoreType.REGULAR, dma, dma((Z,))]

    def call(body, outs, scratch, number):
        return pl.pallas_call(
            body,
            out_shape=outs,
            in_specs=[anywhere] * 3,
            out_specs=(vmem,) * len(outs),
            scratch_shapes=scratch,
            compiler_params=pltpu.CompilerParams(
                collective_id=number, has_side_effects=True, vmem_limit_bytes=48 << 20
            ),
        )(embeddings, labels, ranks)

    best, central, full = call(
        two_hop_kernel,
        (line, line, jax.ShapeDtypeStruct((1, LANES), F32)),
        buffers(DIRECT)
        + [
            pltpu.VMEM((Z, SPILL, width), BF16),
            pltpu.VMEM((Z, SPILL, width), BF16),
            pltpu.VMEM((Z, SPILL, LANES), BF16),
            pltpu.VMEM((Z, SPILL, LANES), BF16),
            pltpu.VMEM((PLANE, Z, HOPPED, width), BF16),
            pltpu.VMEM((PLANE, Z, HOPPED, width), BF16),
        ]
        + sems
        + [dma((3,)), dma((4,)), dma((4,))]
        + [dma] * 6,
        0,
    )

    def again():
        return tuple(call(four_slot_kernel, (line, line), buffers(CAP) + sems + [dma, dma((4,)), dma((4,))], 1))

    return lax.cond(full[0, 0] > 4.0, again, lambda: (best, central))


def solution(mesh):
    placed = (P(("dp", "rep"), None), P(("dp", "rep"), None), P(("dp", "rep"), None, None))
    return jax.shard_map(
        per_device,
        mesh=mesh,
        in_specs=placed,
        out_specs=(P(("dp", "rep"), None), P(("dp", "rep"), None)),
        check_vma=False,
    )
```

```python
import functools

import jax
import jax.numpy as jnp
from jax import lax
from jax.experimental import pallas as pl
from jax.experimental.pallas import tpu as pltpu
from jax.sharding import PartitionSpec as P

MESH = pl.DeviceIdType.MESH
SLOTS = 1024
CAP = 4
DIRECT = 2
HOPPED = CAP - DIRECT
SPILL = 16
Y, Z, X, C = 4, 8, 4, 2
XC = X * C
PLANE = Y * XC
DEVICES = Z * PLANE
SIDE = 16
LANES = 128
EPS = 1e-06
EMPTY = 2.0
FULL = 8.0
ORDER = (0, 1, 7, 2, 6, 4, 3, 5)
EARLY = 5
STRIDE = 13
F32 = jnp.float32
BF16 = jnp.bfloat16


def iota(shape, dim):
    return lax.broadcasted_iota(jnp.int32, shape, dim)


def rows_dot(a, b):
    return lax.dot_general(a, b, (((1,), (1,)), ((), ())), preferred_element_type=F32)


def device(flat):
    return (flat // C, lax.rem(flat, C))


def along_sublanes(row, size):
    turned = jnp.broadcast_to(row, (LANES, row.shape[1])).T
    return jnp.concatenate([turned] * (size // LANES), axis=1)


def earlier_equal(key, size):
    same = (along_sublanes(key, size) == key) & (iota((size, size), 0) < iota((size, size), 1))
    return jnp.sum(jnp.where(same, 1.0, 0.0), axis=0, keepdims=True)


def place():
    dp, core = lax.axis_index("dp"), lax.axis_index("rep")
    return dp * C + core, dp // (Z * X), lax.rem(dp // X, Z), lax.rem(dp, X), core


def row_mate(me, i):
    y, z, x, c = me // (Z * XC), lax.rem(me // XC, Z), lax.rem(me // C, X), lax.rem(me, C)
    return ((y * Z + lax.rem(z + i // C, Z)) * X + x) * C + lax.rem(c + i, C)


def column_mate(me, i):
    y, z, x, c = me // (Z * XC), lax.rem(me // XC, Z), lax.rem(me // C, X), lax.rem(me, C)
    return ((lax.rem(y + i // X, Y) * Z + z) * X + lax.rem(x + i, X)) * C + c


def greet(me):
    barrier = pltpu.get_barrier_semaphore()

    def one(i, _):
        pl.semaphore_signal(barrier, inc=1, device_id=device(row_mate(me, i)), device_id_type=MESH)
        pl.semaphore_signal(barrier, inc=1, device_id=device(column_mate(me, i)), device_id_type=MESH)
        return 0

    lax.fori_loop(1, SIDE, one, 0)


def pass_on(me, stage_sem):
    pl.semaphore_wait(pltpu.get_barrier_semaphore(), 2 * (SIDE - 1))

    def one(i, _):
        pl.semaphore_signal(stage_sem, inc=1, device_id=device(row_mate(me, i)), device_id_type=MESH)
        return 0

    lax.fori_loop(1, SIDE, one, 0)


def fetch(sources, targets, sems):
    copies = [pltpu.make_async_copy(s, t, sems.at[k]) for k, (s, t) in enumerate(zip(sources, targets))]
    for copy in copies:
        copy.start()
    return copies


def normalise(emb_ref, unit):
    rows = emb_ref.shape[0]
    step = 128

    def one(i, _):
        at = pl.ds(pl.multiple_of(i * step, step), step)
        emb = emb_ref[at, :]
        unit[at, :] = (emb * lax.rsqrt(jnp.sum(emb * emb, axis=1, keepdims=True) + EPS)).astype(BF16)
        return 0

    lax.fori_loop(0, rows // step, one, 0)


def build(target, unit, buf, total, per, full=None):
    rows, width = unit.shape
    step = 128

    def one(i, _):
        slot = (iota((step, rows), 0) + i * step).astype(F32)
        chosen = jnp.where(slot == target, 1.0, 0.0)
        some = jnp.sum(chosen, axis=1, keepdims=True)
        block = jnp.dot(chosen.astype(BF16), unit[...], preferred_element_type=F32)
        first = iota((step, width), 1) == 0
        block = jnp.where((some < 0.5) & first, EMPTY, block)
        if full is not None:
            block = jnp.where((full > 0.5) & first, FULL, block)
        buf[pl.ds(i * (step // per), step // per)] = block.astype(BF16).reshape(step // per, per, width)
        return 0

    lax.fori_loop(0, total // step, one, 0)


def turn_picks(bnd_ref, picks):
    bound = bnd_ref.shape[1]
    raw = bnd_ref[...].astype(F32)
    for side in range(2):
        picks[pl.ds(side * bound, bound)] = jnp.broadcast_to(raw[side : side + 1], (LANES, bound)).T


def in_plane(place_of_me, i):
    _, my_y, _, my_x, core = place_of_me
    i = lax.rem(i * STRIDE, PLANE)
    return lax.rem(my_y + i // XC, Y), lax.rem(my_x + i // C, X), lax.rem(core + i, C)


def send_one(place_of_me, dz, i, source, target, send_sem, recv_sem):
    y, x, c = in_plane(place_of_me, i)
    t = (y * Z + lax.rem(place_of_me[2] + dz, Z)) * X + x
    pltpu.make_async_remote_copy(
        source.at[t * C + c], target.at[place_of_me[0]], send_sem, recv_sem.at[dz],
        device_id=(t, c), device_id_type=MESH,
    ).start()


def send_group(place_of_me, dzs, source, target, send_sem, recv_sem, beside=None):
    def one(i, _):
        if beside is not None:
            beside(i)
        for dz in dzs:
            send_one(place_of_me, dz, i, source, target, send_sem, recv_sem)
        return 0

    for dz in dzs:
        if dz:
            send_one(place_of_me, dz, 0, source, target, send_sem, recv_sem)
    lax.fori_loop(1, PLANE, one, 0)


def awaited(me, ref, n, send_sem, recv_sem):
    view = ref.at[pl.ds(0, n)]
    return pltpu.make_async_remote_copy(
        view, view, send_sem, recv_sem, device_id=device(row_mate(me, 1)), device_id_type=MESH
    )


def exchange(me, part, rows, bound, outward, beside, side_send, side_recv):
    half = bound // 2
    side = 1 - part % 2
    at = pl.ds(side * bound + part // 2 * half, half)
    outward[at] = rows
    peer = lax.rem(me + 1, DEVICES) if side == 1 else lax.rem(me + DEVICES - 1, DEVICES)
    copy = pltpu.make_async_remote_copy(
        outward.at[at], beside.at[at], side_send.at[part], side_recv.at[part],
        device_id=device(peer), device_id_type=MESH,
    )
    copy.start()
    return copy, side, at


def filled_slots(members):
    corner = jnp.where(iota((8, LANES), 1) == 0, 1.0, 0.0).astype(BF16)
    heads = rows_dot(corner, members[:, :LANES])[:1]
    return heads, jnp.where(heads < 1.5, 1.0, 0.0)


def close(me, members, filled, sums, copies, beside, best_ref, cent_ref):
    width = members.shape[1]
    table = members[...]
    direction = sums * lax.rsqrt(jnp.sum(sums * sums, axis=1, keepdims=True) + EPS)
    high = direction.astype(BF16)
    rest = direction - high.astype(F32)
    middle = rest.astype(BF16)
    low = (rest - middle.astype(F32)).astype(BF16)
    row = iota((8, width), 0)
    parts = jnp.where(row == 2, low.astype(F32), 0.0)
    parts = jnp.where(row == 1, middle.astype(F32), parts)
    parts = jnp.where(row == 0, high.astype(F32), parts)
    central = jnp.sum(rows_dot(parts.astype(BF16), table), axis=0, keepdims=True)
    cent_ref[...] = jnp.where(filled > 0.5, central, 0.0)

    chunk = 256
    best = jnp.full((8, SLOTS), -1.0, F32)
    for first in range(0, SLOTS, chunk):
        scores = rows_dot(members[first : first + chunk], table)
        empty = members[first : first + chunk, :LANES][:, :1].astype(F32) > 1.5
        barred = empty | (iota((chunk, SLOTS), 0) + first == iota((chunk, SLOTS), 1))
        scores = jnp.where(barred, -1.0, scores)
        best = jnp.maximum(best, jnp.max(scores.reshape(chunk // 8, 8, SLOTS), axis=0))
    for copy, side, at in copies:
        copy.wait()
        scores = rows_dot(beside[at], table)
        top = jnp.max(scores.reshape(at.size // 8, 8, SLOTS), axis=0)
        there = me > 0 if side == 1 else me < DEVICES - 1
        best = jnp.maximum(best, jnp.where(there, top, -1.0))
    nearest = jnp.max(best, axis=0, keepdims=True)
    best_ref[...] = jnp.where(filled > 0.5, nearest, 0.0)


def wrapped(want, count):
    return want - jnp.floor((want + 0.5) / count) * count


def finish(me, members, picks, outward, beside, side_send, side_recv, best_ref, cent_ref):
    bound = outward.shape[0] // 2
    groups = SLOTS // LANES
    _, filled = filled_slots(members)
    stacked = jnp.concatenate([filled[:, k * LANES : (k + 1) * LANES] for k in range(groups)], axis=0)
    upto = jnp.where(iota((LANES, LANES), 0) <= iota((LANES, LANES), 1), 1.0, 0.0).astype(BF16)
    within = jnp.dot(stacked.astype(BF16), upto, preferred_element_type=F32)
    totals = jnp.sum(stacked, axis=1, keepdims=True)
    count = jnp.sum(totals, axis=0, keepdims=True)
    order = []
    before = jnp.zeros((1, 1), F32)
    for k in range(groups):
        order.append(jnp.where(stacked[k : k + 1] > 0.5, within[k : k + 1] + (before - 1.0), -1.0))
        before = before + totals[k : k + 1]
    table = members[...]
    copies = []
    half = bound // 2
    for part in range(4):
        want = wrapped(picks[pl.ds((1 - part % 2) * bound + part // 2 * half, half)], count)
        chosen = [jnp.where(want == order[k], 1.0, 0.0).astype(BF16) for k in range(groups)]
        rows = jnp.dot(jnp.concatenate(chosen, axis=1), table, preferred_element_type=F32).astype(BF16)
        copies.append(exchange(me, part, rows, bound, outward, beside, side_send, side_recv))
    weights = jnp.broadcast_to(filled, (8, SLOTS)).astype(BF16)
    sums = jnp.dot(weights, table, preferred_element_type=F32)[:1]
    close(me, members, filled, sums, copies, beside, best_ref, cent_ref)


def ranked(lab_ref):
    labels = lab_ref[...]
    rows = labels.shape[1]
    return labels, earlier_equal(labels.astype(F32), rows)


def four_slot_kernel(
    emb_hbm, lab_hbm, bnd_hbm, best_ref, cent_ref,
    emb_ref, lab_ref, bnd_ref, unit, out_buf, in_buf, members, picks, outward, beside,
    in_sem, stage_sem, send_sem, recv_sem, own_sem, side_send, side_recv,
):
    width = emb_ref.shape[1]
    here = place()
    me, _, my_z, _, _ = here
    got = fetch((emb_hbm, lab_hbm, bnd_hbm), (emb_ref, lab_ref, bnd_ref), in_sem)
    greet(me)
    for copy in got:
        copy.wait()
    labels, rank = ranked(lab_ref)
    normalise(emb_ref, unit)
    pass_on(me, stage_sem)
    build(labels.astype(F32) * CAP + rank, unit, out_buf, SLOTS, CAP)
    pl.semaphore_wait(stage_sem, SIDE - 1)
    own = pltpu.make_async_copy(out_buf.at[me], in_buf.at[me], own_sem)
    own.start()
    for dz in ORDER:
        send_group(here, (dz,), out_buf, in_buf, send_sem, recv_sem)
    turn_picks(bnd_ref, picks)
    own.wait()
    for dz in ORDER:
        awaited(me, in_buf, PLANE - 1 if dz == 0 else PLANE, send_sem, recv_sem.at[dz]).wait_recv()
        z = lax.rem(my_z + Z - dz, Z)
        for y in range(Y):
            first = (y * Z + z) * XC
            members[pl.ds(pl.multiple_of(first * CAP, XC * CAP), XC * CAP)] = in_buf[pl.ds(first, XC)].reshape(
                XC * CAP, width
            )
    finish(me, members, picks, outward, beside, side_send, side_recv, best_ref, cent_ref)
    awaited(me, out_buf, DEVICES - 1, send_sem, recv_sem.at[0]).wait_send()


def two_hop_kernel(
    emb_hbm, lab_hbm, bnd_hbm, best_ref, cent_ref, full_ref,
    emb_ref, lab_ref, bnd_ref, unit, out_buf, in_buf, members, picks, outward, beside,
    out_spill, in_spill, out_code, in_code, out_hop, in_hop, out_count, in_count, direct_pick, hop_pick, acc, direct,
    in_sem, stage_sem, send_sem, recv_sem, own_sem, side_send, side_recv,
    spill_send, spill_recv, code_send, code_recv, hop_send, hop_recv, count_send, count_recv,
):
    rows, width = emb_ref.shape
    here = place()
    me, my_y, my_z, my_x, core = here
    mine = (my_y * X + my_x) * C + core
    got = fetch((emb_hbm, lab_hbm, bnd_hbm), (emb_ref, lab_ref, bnd_ref), in_sem)
    greet(me)
    got[1].wait()
    labels, rank = ranked(lab_ref)
    spilled = rank > DIRECT - 0.5
    plane = (labels >> 3) & (Z - 1)
    within = ((labels >> 6) << 3) | (labels & (XC - 1))
    key = jnp.where(spilled, plane, Z).astype(F32)
    spot = earlier_equal(key, rows)
    fits = spilled & (spot < SPILL - 0.5)
    full = jnp.max(jnp.where(spilled & (spot > SPILL - 0.5), 1.0, 0.0), axis=1, keepdims=True)
    direct_at = jnp.where(spilled, -1.0, labels.astype(F32) * DIRECT + rank)
    spill_at = jnp.where(fits, plane.astype(F32) * SPILL + spot, -1.0)
    code = within.astype(F32) * HOPPED + rank + (1 - DIRECT)
    pass_on(me, stage_sem)
    got[0].wait()
    normalise(emb_ref, unit)

    lines = Z * SPILL
    chosen = jnp.where(iota((lines, rows), 0).astype(F32) == spill_at, 1.0, 0.0)
    out_spill[...] = (
        jnp.dot(chosen.astype(BF16), unit[...], preferred_element_type=F32).astype(BF16).reshape(Z, SPILL, width)
    )
    lane = iota((rows, LANES), 1).astype(F32)
    by_spot = jnp.where(along_sublanes(spot, LANES) == lane, 1.0, 0.0).astype(BF16)
    by_owner = jnp.where(along_sublanes(within.astype(F32), LANES) + PLANE == lane, 1.0, 0.0).astype(BF16)
    here_z = iota((Z, rows), 0) == plane
    coded = jnp.where(here_z & fits, code, 0.0).astype(BF16)
    counted = jnp.where(here_z, 1.0, 0.0).astype(BF16)
    info = jnp.dot(coded, by_spot, preferred_element_type=F32)
    info = info + jnp.dot(counted, by_owner, preferred_element_type=F32)
    out_code[...] = jnp.broadcast_to(info[:, None, :], (Z, 8, LANES)).astype(BF16)

    def over(i, _):
        z = lax.rem(my_z + i, Z)
        to = ((my_y * Z + z) * X + my_x, core)
        pltpu.make_async_remote_copy(
            out_code.at[z], in_code.at[my_z], code_send, code_recv, device_id=to, device_id_type=MESH
        ).start()
        pltpu.make_async_remote_copy(
            out_spill.at[z], in_spill.at[my_z], spill_send, spill_recv, device_id=to, device_id_type=MESH
        ).start()
        return 0

    lax.fori_loop(1, Z, over, 0)
    build(direct_at, unit, out_buf, DEVICES * DIRECT, DIRECT, full)
    pl.semaphore_wait(stage_sem, SIDE - 1)
    own = fetch(
        (out_buf.at[me], out_spill.at[my_z], out_code.at[my_z]),
        (in_buf.at[me], in_spill.at[my_z], in_code.at[my_z]),
        own_sem,
    )
    send_group(here, ORDER[:EARLY], out_buf, in_buf, send_sem, recv_sem)
    got[2].wait()
    turn_picks(bnd_ref, picks)
    for copy in own:
        copy.wait()

    awaited(me, in_code, Z - 1, code_send, code_recv).wait_recv()
    awaited(me, in_spill, Z - 1, spill_send, spill_recv).wait_recv()
    info = jnp.max(in_code[...].astype(F32), axis=1)
    turned = jnp.concatenate([info] * (LANES // Z), axis=0).T[PLANE : 2 * PLANE]
    out_count[...] = jnp.broadcast_to(turned[:, None, :], (PLANE, 8, LANES)).astype(BF16)

    def tell(i, _):
        y, x, c = in_plane(here, i)
        pltpu.make_async_remote_copy(
            out_count.at[(y * X + x) * C + c], in_count.at[mine], count_send, count_recv,
            device_id=((y * Z + my_z) * X + x, c), device_id_type=MESH,
        ).start()
        return 0

    lax.fori_loop(1, PLANE, tell, 0)
    noted = pltpu.make_async_copy(out_count.at[mine], in_count.at[mine], own_sem.at[1])
    noted.start()
    spread = jnp.where(iota((LANES, LANES), 0) == (iota((LANES, LANES), 1) & (SPILL - 1)), 1.0, 0.0).astype(BF16)
    told = jnp.dot(info.astype(BF16), spread, preferred_element_type=F32)
    told = jnp.sum(jnp.where(iota((Z, LANES), 0) == (iota((Z, LANES), 1) >> 4), told, 0.0), axis=0, keepdims=True)
    owner = jnp.floor((told - 0.5) * (1.0 / HOPPED))
    line = owner * (Z * HOPPED) + (iota((1, lines), 1) >> 4).astype(F32) * HOPPED + (told - 1.0 - owner * HOPPED)
    line = jnp.where(told > 0.5, line, -1.0)
    came = in_spill[...].reshape(lines, width)
    step = 128
    for i in range(PLANE * Z * HOPPED // step):
        chosen = jnp.where((iota((step, lines), 0) + i * step).astype(F32) == line, 1.0, 0.0)
        some = jnp.sum(chosen, axis=1, keepdims=True)
        block = jnp.dot(chosen.astype(BF16), came, preferred_element_type=F32)
        block = jnp.where((some < 0.5) & (iota((step, width), 1) == 0), EMPTY, block)
        each = Z * HOPPED
        out_hop[pl.ds(i * (step // each), step // each)] = block.astype(BF16).reshape(step // each, each, width)

    def around(i):
        y, x, c = in_plane(here, i)
        pltpu.make_async_remote_copy(
            out_hop.at[(y * X + x) * C + c], in_hop.at[mine], hop_send, hop_recv,
            device_id=((y * Z + my_z) * X + x, c), device_id_type=MESH,
        ).start()

    kept = pltpu.make_async_copy(out_hop.at[mine], in_hop.at[mine], own_sem.at[0])
    kept.start()
    send_group(here, ORDER[EARLY:], out_buf, in_buf, send_sem, recv_sem, around)
    kept.wait()
    noted.wait()

    awaited(me, in_count, PLANE - 1, count_send, count_recv).wait_recv()
    bound = outward.shape[0] // 2
    counts = jnp.max(in_count[...].astype(F32), axis=1)
    a, b = iota((PLANE, PLANE), 0), iota((PLANE, PLANE), 1)
    j, m = iota((LANES, LANES), 0), iota((LANES, LANES), 1)

    def ones(mask):
        return jnp.where(mask, 1.0, 0.0)

    def small(left, right):
        return jnp.dot(left.astype(BF16), right.astype(BF16), preferred_element_type=F32)

    def exact(left, right):
        return jnp.dot(left, right, precision=lax.Precision.HIGHEST, preferred_element_type=F32)

    same_y = (a >> 3) == (b >> 3)
    base = small(ones(same_y & (b < a)), counts)
    base = base + small(small(ones(same_y), counts), ones((j < Z) & (j < (m & (Z - 1)))))
    base = base + small(small(ones((b >> 3) < (a >> 3)), counts), ones(j < Z))
    count = jnp.sum(jnp.where(iota((PLANE, LANES), 1) < Z, counts, 0.0), axis=1, keepdims=True)
    count = jnp.sum(count, axis=0, keepdims=True)
    want = wrapped(picks[...], count)

    def standing(array):
        return jnp.concatenate([array, jnp.zeros((LANES - PLANE, LANES), F32)], axis=0).T[:Z]

    widen = ones((j == (m >> 1)) & (m < PLANE * DIRECT))
    rank = (iota((Z, LANES), 1) & (DIRECT - 1)).astype(F32)
    taken = rank < small(standing(counts), widen) - 0.5
    order = jnp.where(taken, exact(standing(base), widen) + rank, -1.0)
    taken = ones(taken)
    for z in range(Z):
        direct_pick[z, pl.ds(0, 2 * bound)] = ones(want == order[z : z + 1]).astype(BF16)
        direct_pick[z, pl.ds(2 * bound, 16)] = jnp.broadcast_to(taken[z : z + 1], (16, LANES)).astype(BF16)

    from_z = ones(j == ((m >> 1) & (Z - 1)))
    own_xc = (iota((PLANE, LANES), 0) & (XC - 1)) == (iota((PLANE, LANES), 1) >> 4)

    def folded(array):
        return jnp.sum(jnp.where(own_xc, array, 0.0).reshape(Y, XC, LANES), axis=1)

    rank = (iota((Y, LANES), 1) & (HOPPED - 1)).astype(F32) + DIRECT
    taken = rank < folded(small(counts, from_z)) - 0.5
    order = jnp.where(taken, folded(exact(base, from_z)) + rank, -1.0)
    taken = ones(taken)
    for y in range(Y):
        at = pl.ds(y * LANES, LANES)
        hop_pick[pl.ds(0, 2 * bound), at] = ones(want == order[y : y + 1]).astype(BF16)
        hop_pick[pl.ds(2 * bound, 16), at] = jnp.broadcast_to(taken[y : y + 1], (16, LANES)).astype(BF16)

    each = PLANE * DIRECT

    def settle(dz):
        awaited(me, in_buf, PLANE - 1 if dz == 0 else PLANE, send_sem, recv_sem.at[dz]).wait_recv()
        z = lax.rem(my_z + Z - dz, Z)
        for y in range(Y):
            direct[z, pl.ds(y * XC * DIRECT, XC * DIRECT)] = in_buf[pl.ds((y * Z + z) * XC, XC)].reshape(
                XC * DIRECT, width
            )
        return z

    for n, dz in enumerate(ORDER[:EARLY]):
        z = settle(dz)
        given = jnp.dot(direct_pick[z][:, :each], direct[z], preferred_element_type=F32)
        acc[...] = given if n == 0 else acc[...] + given
    awaited(me, in_hop, PLANE - 1, hop_send, hop_recv).wait_recv()
    hopped = in_hop[...].reshape(PLANE * Z * HOPPED, width)
    acc[...] += jnp.dot(hop_pick[...], hopped, preferred_element_type=F32)
    planes = [settle(dz) for dz in ORDER[EARLY:]]
    latest = jnp.concatenate([direct[z] for z in planes], axis=0)

    def gather(first, size):
        at = pl.ds(first, size)
        chosen = jnp.concatenate([direct_pick[z, at][:, :each] for z in planes], axis=1)
        return acc[at] + jnp.dot(chosen, latest, preferred_element_type=F32)

    half = bound // 2
    copies = []
    for part in range(4):
        rows_out = gather((1 - part % 2) * bound + part // 2 * half, half).astype(BF16)
        copies.append(exchange(me, part, rows_out, bound, outward, beside, side_send, side_recv))
    sums = gather(2 * bound, 16)[:1]

    lines = PLANE * CAP
    a, b = iota((lines, each), 0), iota((lines, each), 1)
    k = a & (CAP - 1)
    from_direct = ones((k < DIRECT) & (b == (a >> 2) * DIRECT + k)).astype(BF16)
    a, b = iota((lines, PLANE * Z * HOPPED), 0), iota((lines, PLANE * Z * HOPPED), 1)
    k = a & (CAP - 1)
    for z in range(Z):
        from_hop = ones((k >= DIRECT) & (b == (a >> 2) * (Z * HOPPED) + z * HOPPED + k - DIRECT)).astype(BF16)
        mixed = jnp.dot(from_direct, direct[z], preferred_element_type=F32)
        mixed = (mixed + jnp.dot(from_hop, hopped, preferred_element_type=F32)).astype(BF16)
        for y in range(Y):
            members[pl.ds((y * Z + z) * XC * CAP, XC * CAP)] = mixed[y * XC * CAP : (y + 1) * XC * CAP]
    heads, filled = filled_slots(members)
    close(me, members, filled, sums, copies, beside, best_ref, cent_ref)
    full_ref[...] = jnp.broadcast_to(jnp.max(heads, axis=1, keepdims=True), full_ref.shape)

    awaited(me, out_buf, DEVICES - 1, send_sem, recv_sem.at[0]).wait_send()
    awaited(me, out_spill, Z - 1, spill_send, spill_recv).wait_send()
    awaited(me, out_code, Z - 1, code_send, code_recv).wait_send()
    awaited(me, out_hop, PLANE - 1, hop_send, hop_recv).wait_send()
    awaited(me, out_count, PLANE - 1, count_send, count_recv).wait_send()


def per_device(embeddings, cluster_ids, boundary_slots):
    rows, width = embeddings.shape
    bound = boundary_slots.shape[2]
    labels, ranks = cluster_ids.reshape(1, rows), boundary_slots[0]
    line = jax.ShapeDtypeStruct((1, SLOTS), F32)
    vmem, anywhere = pl.BlockSpec(memory_space=pltpu.VMEM), pl.BlockSpec(memory_space=pl.ANY)
    dma = pltpu.SemaphoreType.DMA

    def buffers(per):
        return [
            pltpu.VMEM((rows, width), F32),
            pltpu.VMEM((1, rows), jnp.int32),
            pltpu.VMEM((2, bound), jnp.int32),
            pltpu.VMEM((rows, width), BF16),
            pltpu.VMEM((DEVICES, per, width), BF16),
            pltpu.VMEM((DEVICES, per, width), BF16),
            pltpu.VMEM((SLOTS, width), BF16),
            pltpu.VMEM((2 * bound, LANES), F32),
            pltpu.VMEM((2 * bound, width), BF16),
            pltpu.VMEM((2 * bound, width), BF16),
        ]

    sems = [dma((3,)), pltpu.SemaphoreType.REGULAR, dma, dma((Z,))]

    def call(body, outs, scratch, number):
        return pl.pallas_call(
            body,
            out_shape=outs,
            in_specs=[anywhere] * 3,
            out_specs=(vmem,) * len(outs),
            scratch_shapes=scratch,
            compiler_params=pltpu.CompilerParams(
                collective_id=number, has_side_effects=True, vmem_limit_bytes=48 << 20
            ),
        )(embeddings, labels, ranks)

    best, central, full = call(
        two_hop_kernel,
        (line, line, jax.ShapeDtypeStruct((1, LANES), F32)),
        buffers(DIRECT)
        + [
            pltpu.VMEM((Z, SPILL, width), BF16),
            pltpu.VMEM((Z, SPILL, width), BF16),
            pltpu.VMEM((Z, 8, LANES), BF16),
            pltpu.VMEM((Z, 8, LANES), BF16),
            pltpu.VMEM((PLANE, Z * HOPPED, width), BF16),
            pltpu.VMEM((PLANE, Z * HOPPED, width), BF16),
            pltpu.VMEM((PLANE, 8, LANES), BF16),
            pltpu.VMEM((PLANE, 8, LANES), BF16),
            pltpu.VMEM((Z, 2 * bound + 16, LANES), BF16),
            pltpu.VMEM((2 * bound + 16, PLANE * Z * HOPPED), BF16),
            pltpu.VMEM((2 * bound + 16, width), F32),
            pltpu.VMEM((Z, PLANE * DIRECT, width), BF16),
        ]
        + sems
        + [dma((3,)), dma((4,)), dma((4,))]
        + [dma] * 8,
        0,
    )

    def again():
        return tuple(call(four_slot_kernel, (line, line), buffers(CAP) + sems + [dma, dma((4,)), dma((4,))], 1))

    return lax.cond(full[0, 0] > 4.0, again, lambda: (best, central))


def solution(mesh):
    placed = (P(("dp", "rep"), None), P(("dp", "rep"), None), P(("dp", "rep"), None, None))
    return jax.shard_map(
        per_device,
        mesh=mesh,
        in_specs=placed,
        out_specs=(P(("dp", "rep"), None), P(("dp", "rep"), None)),
        check_vma=False,
    )
```

```python
import functools

import jax
import jax.numpy as jnp
from jax import lax
from jax.experimental import pallas as pl
from jax.experimental.pallas import tpu as pltpu
from jax.sharding import PartitionSpec as P

MESH = pl.DeviceIdType.MESH
SLOTS = 1024
CAP = 4
DIRECT = 2
HOPPED = CAP - DIRECT
SPILL = 16
Y, Z, X, C = 4, 8, 4, 2
XC = X * C
PLANE = Y * XC
DEVICES = Z * PLANE
SIDE = 16
LANES = 128
EPS = 1e-06
EMPTY = 2.0
FULL = 8.0
ORDER = (0, 1, 7, 2, 6, 4, 3, 5)
EARLY = 5
STRIDE = 13
F32 = jnp.float32
BF16 = jnp.bfloat16


def iota(shape, dim):
    return lax.broadcasted_iota(jnp.int32, shape, dim)


def rows_dot(a, b):
    return lax.dot_general(a, b, (((1,), (1,)), ((), ())), preferred_element_type=F32)


def device(flat):
    return (flat // C, lax.rem(flat, C))


def along_sublanes(row, size):
    turned = jnp.broadcast_to(row, (LANES, row.shape[1])).T
    return jnp.concatenate([turned] * (size // LANES), axis=1)


def earlier_equal(key, size):
    same = (along_sublanes(key, size) == key) & (iota((size, size), 0) < iota((size, size), 1))
    return jnp.sum(jnp.where(same, 1.0, 0.0), axis=0, keepdims=True)


def place():
    dp, core = lax.axis_index("dp"), lax.axis_index("rep")
    return dp * C + core, dp // (Z * X), lax.rem(dp // X, Z), lax.rem(dp, X), core


def row_mate(me, i):
    y, z, x, c = me // (Z * XC), lax.rem(me // XC, Z), lax.rem(me // C, X), lax.rem(me, C)
    return ((y * Z + lax.rem(z + i // C, Z)) * X + x) * C + lax.rem(c + i, C)


def column_mate(me, i):
    y, z, x, c = me // (Z * XC), lax.rem(me // XC, Z), lax.rem(me // C, X), lax.rem(me, C)
    return ((lax.rem(y + i // X, Y) * Z + z) * X + lax.rem(x + i, X)) * C + c


def greet(me):
    barrier = pltpu.get_barrier_semaphore()

    def one(i, _):
        pl.semaphore_signal(barrier, inc=1, device_id=device(row_mate(me, i)), device_id_type=MESH)
        pl.semaphore_signal(barrier, inc=1, device_id=device(column_mate(me, i)), device_id_type=MESH)
        return 0

    lax.fori_loop(1, SIDE, one, 0)


def pass_on(me, stage_sem):
    pl.semaphore_wait(pltpu.get_barrier_semaphore(), 2 * (SIDE - 1))

    def one(i, _):
        pl.semaphore_signal(stage_sem, inc=1, device_id=device(row_mate(me, i)), device_id_type=MESH)
        return 0

    lax.fori_loop(1, SIDE, one, 0)


def fetch(sources, targets, sems):
    copies = [pltpu.make_async_copy(s, t, sems.at[k]) for k, (s, t) in enumerate(zip(sources, targets))]
    for copy in copies:
        copy.start()
    return copies


def normalise(emb_ref, unit):
    rows = emb_ref.shape[0]
    step = 128

    def one(i, _):
        at = pl.ds(pl.multiple_of(i * step, step), step)
        emb = emb_ref[at, :]
        unit[at, :] = (emb * lax.rsqrt(jnp.sum(emb * emb, axis=1, keepdims=True) + EPS)).astype(BF16)
        return 0

    lax.fori_loop(0, rows // step, one, 0)


def build(target, unit, buf, total, per, full=None):
    rows, width = unit.shape
    step = 128

    def one(i, _):
        slot = (iota((step, rows), 0) + i * step).astype(F32)
        chosen = jnp.where(slot == target, 1.0, 0.0)
        some = jnp.sum(chosen, axis=1, keepdims=True)
        block = jnp.dot(chosen.astype(BF16), unit[...], preferred_element_type=F32)
        first = iota((step, width), 1) == 0
        block = jnp.where((some < 0.5) & first, EMPTY, block)
        if full is not None:
            block = jnp.where((full > 0.5) & first, FULL, block)
        buf[pl.ds(i * (step // per), step // per)] = block.astype(BF16).reshape(step // per, per, width)
        return 0

    lax.fori_loop(0, total // step, one, 0)


def turn_picks(bnd_ref, picks):
    bound = bnd_ref.shape[1]
    raw = bnd_ref[...].astype(F32)
    for side in range(2):
        picks[pl.ds(side * bound, bound)] = jnp.broadcast_to(raw[side : side + 1], (LANES, bound)).T


def in_plane(place_of_me, i):
    _, my_y, _, my_x, core = place_of_me
    i = lax.rem(i * STRIDE, PLANE)
    return lax.rem(my_y + i // XC, Y), lax.rem(my_x + i // C, X), lax.rem(core + i, C)


def send_one(place_of_me, dz, i, source, target, send_sem, recv_sem):
    y, x, c = in_plane(place_of_me, i)
    t = (y * Z + lax.rem(place_of_me[2] + dz, Z)) * X + x
    pltpu.make_async_remote_copy(
        source.at[t * C + c], target.at[place_of_me[0]], send_sem, recv_sem.at[dz],
        device_id=(t, c), device_id_type=MESH,
    ).start()


def send_group(place_of_me, dzs, source, target, send_sem, recv_sem, beside=None):
    def one(i, _):
        if beside is not None:
            beside(i)
        for dz in dzs:
            send_one(place_of_me, dz, i, source, target, send_sem, recv_sem)
        return 0

    for dz in dzs:
        if dz:
            send_one(place_of_me, dz, 0, source, target, send_sem, recv_sem)
    lax.fori_loop(1, PLANE, one, 0)


def awaited(me, ref, n, send_sem, recv_sem):
    view = ref.at[pl.ds(0, n)]
    return pltpu.make_async_remote_copy(
        view, view, send_sem, recv_sem, device_id=device(row_mate(me, 1)), device_id_type=MESH
    )


def exchange(me, part, rows, bound, outward, beside, side_send, side_recv):
    half = bound // 2
    side = 1 - part % 2
    at = pl.ds(side * bound + part // 2 * half, half)
    outward[at] = rows
    peer = lax.rem(me + 1, DEVICES) if side == 1 else lax.rem(me + DEVICES - 1, DEVICES)
    copy = pltpu.make_async_remote_copy(
        outward.at[at], beside.at[at], side_send.at[part], side_recv.at[part],
        device_id=device(peer), device_id_type=MESH,
    )
    copy.start()
    return copy, side, at


def filled_slots(members):
    corner = jnp.where(iota((8, LANES), 1) == 0, 1.0, 0.0).astype(BF16)
    heads = rows_dot(corner, members[:, :LANES])[:1]
    return heads, jnp.where(heads < 1.5, 1.0, 0.0)


def close(me, members, filled, sums, copies, beside, best_ref, cent_ref):
    width = members.shape[1]
    table = members[...]
    direction = sums * lax.rsqrt(jnp.sum(sums * sums, axis=1, keepdims=True) + EPS)
    high = direction.astype(BF16)
    rest = direction - high.astype(F32)
    middle = rest.astype(BF16)
    low = (rest - middle.astype(F32)).astype(BF16)
    row = iota((8, width), 0)
    parts = jnp.where(row == 2, low.astype(F32), 0.0)
    parts = jnp.where(row == 1, middle.astype(F32), parts)
    parts = jnp.where(row == 0, high.astype(F32), parts)
    central = jnp.sum(rows_dot(parts.astype(BF16), table), axis=0, keepdims=True)
    cent_ref[...] = jnp.where(filled > 0.5, central, 0.0)

    chunk = 256
    best = jnp.full((8, SLOTS), -1.0, F32)
    for first in range(0, SLOTS, chunk):
        scores = rows_dot(members[first : first + chunk], table)
        empty = members[first : first + chunk, :LANES][:, :1].astype(F32) > 1.5
        barred = empty | (iota((chunk, SLOTS), 0) + first == iota((chunk, SLOTS), 1))
        scores = jnp.where(barred, -1.0, scores)
        best = jnp.maximum(best, jnp.max(scores.reshape(chunk // 8, 8, SLOTS), axis=0))
    for copy, side, at in copies:
        copy.wait()
        scores = rows_dot(beside[at], table)
        top = jnp.max(scores.reshape(at.size // 8, 8, SLOTS), axis=0)
        there = me > 0 if side == 1 else me < DEVICES - 1
        best = jnp.maximum(best, jnp.where(there, top, -1.0))
    nearest = jnp.max(best, axis=0, keepdims=True)
    best_ref[...] = jnp.where(filled > 0.5, nearest, 0.0)


def wrapped(want, count):
    return want - jnp.floor((want + 0.5) / count) * count


def finish(me, members, picks, outward, beside, side_send, side_recv, best_ref, cent_ref):
    bound = outward.shape[0] // 2
    groups = SLOTS // LANES
    _, filled = filled_slots(members)
    stacked = jnp.concatenate([filled[:, k * LANES : (k + 1) * LANES] for k in range(groups)], axis=0)
    upto = jnp.where(iota((LANES, LANES), 0) <= iota((LANES, LANES), 1), 1.0, 0.0).astype(BF16)
    within = jnp.dot(stacked.astype(BF16), upto, preferred_element_type=F32)
    totals = jnp.sum(stacked, axis=1, keepdims=True)
    count = jnp.sum(totals, axis=0, keepdims=True)
    order = []
    before = jnp.zeros((1, 1), F32)
    for k in range(groups):
        order.append(jnp.where(stacked[k : k + 1] > 0.5, within[k : k + 1] + (before - 1.0), -1.0))
        before = before + totals[k : k + 1]
    table = members[...]
    copies = []
    half = bound // 2
    for part in range(4):
        want = wrapped(picks[pl.ds((1 - part % 2) * bound + part // 2 * half, half)], count)
        chosen = [jnp.where(want == order[k], 1.0, 0.0).astype(BF16) for k in range(groups)]
        rows = jnp.dot(jnp.concatenate(chosen, axis=1), table, preferred_element_type=F32).astype(BF16)
        copies.append(exchange(me, part, rows, bound, outward, beside, side_send, side_recv))
    weights = jnp.broadcast_to(filled, (8, SLOTS)).astype(BF16)
    sums = jnp.dot(weights, table, preferred_element_type=F32)[:1]
    close(me, members, filled, sums, copies, beside, best_ref, cent_ref)


def ranked(lab_ref):
    labels = lab_ref[...]
    rows = labels.shape[1]
    return labels, earlier_equal(labels.astype(F32), rows)


def four_slot_kernel(
    emb_hbm, lab_hbm, bnd_hbm, best_ref, cent_ref,
    emb_ref, lab_ref, bnd_ref, unit, out_buf, in_buf, members, picks, outward, beside,
    in_sem, stage_sem, send_sem, recv_sem, own_sem, side_send, side_recv,
):
    width = emb_ref.shape[1]
    here = place()
    me, _, my_z, _, _ = here
    got = fetch((emb_hbm, lab_hbm, bnd_hbm), (emb_ref, lab_ref, bnd_ref), in_sem)
    greet(me)
    for copy in got:
        copy.wait()
    labels, rank = ranked(lab_ref)
    normalise(emb_ref, unit)
    pass_on(me, stage_sem)
    build(labels.astype(F32) * CAP + rank, unit, out_buf, SLOTS, CAP)
    pl.semaphore_wait(stage_sem, SIDE - 1)
    own = pltpu.make_async_copy(out_buf.at[me], in_buf.at[me], own_sem)
    own.start()
    for dz in ORDER:
        send_group(here, (dz,), out_buf, in_buf, send_sem, recv_sem)
    turn_picks(bnd_ref, picks)
    own.wait()
    for dz in ORDER:
        awaited(me, in_buf, PLANE - 1 if dz == 0 else PLANE, send_sem, recv_sem.at[dz]).wait_recv()
        z = lax.rem(my_z + Z - dz, Z)
        for y in range(Y):
            first = (y * Z + z) * XC
            members[pl.ds(pl.multiple_of(first * CAP, XC * CAP), XC * CAP)] = in_buf[pl.ds(first, XC)].reshape(
                XC * CAP, width
            )
    finish(me, members, picks, outward, beside, side_send, side_recv, best_ref, cent_ref)
    awaited(me, out_buf, DEVICES - 1, send_sem, recv_sem.at[0]).wait_send()


def two_hop_kernel(
    emb_hbm, lab_hbm, bnd_hbm, best_ref, cent_ref, full_ref,
    emb_ref, lab_ref, bnd_ref, unit, out_buf, in_buf, members, picks, outward, beside,
    out_spill, in_spill, out_code, in_code, out_hop, in_hop, out_count, in_count, direct_pick, hop_pick, acc, direct,
    in_sem, stage_sem, send_sem, recv_sem, own_sem, side_send, side_recv,
    spill_send, spill_recv, code_send, code_recv, hop_send, hop_recv, count_send, count_recv,
):
    rows, width = emb_ref.shape
    here = place()
    me, my_y, my_z, my_x, core = here
    mine = (my_y * X + my_x) * C + core
    got = fetch((emb_hbm, lab_hbm, bnd_hbm), (emb_ref, lab_ref, bnd_ref), in_sem)
    greet(me)
    got[1].wait()
    labels, rank = ranked(lab_ref)
    spilled = rank > DIRECT - 0.5
    plane = (labels >> 3) & (Z - 1)
    within = ((labels >> 6) << 3) | (labels & (XC - 1))
    key = jnp.where(spilled, plane, Z).astype(F32)
    spot = earlier_equal(key, rows)
    fits = spilled & (spot < SPILL - 0.5)
    full = jnp.max(jnp.where(spilled & (spot > SPILL - 0.5), 1.0, 0.0), axis=1, keepdims=True)
    direct_at = jnp.where(spilled, -1.0, labels.astype(F32) * DIRECT + rank)
    spill_at = jnp.where(fits, plane.astype(F32) * SPILL + spot, -1.0)
    code = within.astype(F32) * HOPPED + rank + (1 - DIRECT)
    got[0].wait()
    normalise(emb_ref, unit)

    lines = Z * SPILL
    chosen = jnp.where(iota((lines, rows), 0).astype(F32) == spill_at, 1.0, 0.0)
    out_spill[...] = (
        jnp.dot(chosen.astype(BF16), unit[...], preferred_element_type=F32).astype(BF16).reshape(Z, SPILL, width)
    )
    lane = iota((rows, LANES), 1).astype(F32)
    by_spot = jnp.where(along_sublanes(spot, LANES) == lane, 1.0, 0.0).astype(BF16)
    by_owner = jnp.where(along_sublanes(within.astype(F32), LANES) + PLANE == lane, 1.0, 0.0).astype(BF16)
    here_z = iota((Z, rows), 0) == plane
    coded = jnp.where(here_z & fits, code, 0.0).astype(BF16)
    counted = jnp.where(here_z, 1.0, 0.0).astype(BF16)
    info = jnp.dot(coded, by_spot, preferred_element_type=F32)
    info = info + jnp.dot(counted, by_owner, preferred_element_type=F32)
    out_code[...] = jnp.broadcast_to(info[:, None, :], (Z, 8, LANES)).astype(BF16)
    pass_on(me, stage_sem)

    def over(dz):
        z = lax.rem(my_z + dz, Z)
        to = ((my_y * Z + z) * X + my_x, core)
        pltpu.make_async_remote_copy(
            out_code.at[z], in_code.at[my_z], code_send, code_recv, device_id=to, device_id_type=MESH
        ).start()
        pltpu.make_async_remote_copy(
            out_spill.at[z], in_spill.at[my_z], spill_send, spill_recv, device_id=to, device_id_type=MESH
        ).start()

    for dz in (4, 3, 5, 2, 6, 1, 7):
        over(dz)
    build(direct_at, unit, out_buf, DEVICES * DIRECT, DIRECT, full)
    pl.semaphore_wait(stage_sem, SIDE - 1)
    own = fetch(
        (out_buf.at[me], out_spill.at[my_z], out_code.at[my_z]),
        (in_buf.at[me], in_spill.at[my_z], in_code.at[my_z]),
        own_sem,
    )
    send_group(here, ORDER[:EARLY], out_buf, in_buf, send_sem, recv_sem)
    got[2].wait()
    turn_picks(bnd_ref, picks)
    for copy in own:
        copy.wait()

    awaited(me, in_code, Z - 1, code_send, code_recv).wait_recv()
    awaited(me, in_spill, Z - 1, spill_send, spill_recv).wait_recv()
    info = jnp.max(in_code[...].astype(F32), axis=1)
    turned = jnp.concatenate([info] * (LANES // Z), axis=0).T[PLANE : 2 * PLANE]
    out_count[...] = jnp.broadcast_to(turned[:, None, :], (PLANE, 8, LANES)).astype(BF16)

    def tell(i, _):
        y, x, c = in_plane(here, i)
        pltpu.make_async_remote_copy(
            out_count.at[(y * X + x) * C + c], in_count.at[mine], count_send, count_recv,
            device_id=((y * Z + my_z) * X + x, c), device_id_type=MESH,
        ).start()
        return 0

    lax.fori_loop(1, PLANE, tell, 0)
    noted = pltpu.make_async_copy(out_count.at[mine], in_count.at[mine], own_sem.at[1])
    noted.start()
    spread = jnp.where(iota((LANES, LANES), 0) == (iota((LANES, LANES), 1) & (SPILL - 1)), 1.0, 0.0).astype(BF16)
    told = jnp.dot(info.astype(BF16), spread, preferred_element_type=F32)
    told = jnp.sum(jnp.where(iota((Z, LANES), 0) == (iota((Z, LANES), 1) >> 4), told, 0.0), axis=0, keepdims=True)
    owner = jnp.floor((told - 0.5) * (1.0 / HOPPED))
    line = owner * (Z * HOPPED) + (iota((1, lines), 1) >> 4).astype(F32) * HOPPED + (told - 1.0 - owner * HOPPED)
    line = jnp.where(told > 0.5, line, -1.0)
    came = in_spill[...].reshape(lines, width)
    step = 128
    for i in range(PLANE * Z * HOPPED // step):
        chosen = jnp.where((iota((step, lines), 0) + i * step).astype(F32) == line, 1.0, 0.0)
        some = jnp.sum(chosen, axis=1, keepdims=True)
        block = jnp.dot(chosen.astype(BF16), came, preferred_element_type=F32)
        block = jnp.where((some < 0.5) & (iota((step, width), 1) == 0), EMPTY, block)
        each = Z * HOPPED
        out_hop[pl.ds(i * (step // each), step // each)] = block.astype(BF16).reshape(step // each, each, width)

    def around(i):
        y, x, c = in_plane(here, i)
        pltpu.make_async_remote_copy(
            out_hop.at[(y * X + x) * C + c], in_hop.at[mine], hop_send, hop_recv,
            device_id=((y * Z + my_z) * X + x, c), device_id_type=MESH,
        ).start()

    kept = pltpu.make_async_copy(out_hop.at[mine], in_hop.at[mine], own_sem.at[0])
    kept.start()
    send_group(here, ORDER[EARLY:], out_buf, in_buf, send_sem, recv_sem, around)
    kept.wait()
    noted.wait()

    awaited(me, in_count, PLANE - 1, count_send, count_recv).wait_recv()
    bound = outward.shape[0] // 2
    counts = jnp.max(in_count[...].astype(F32), axis=1)
    a, b = iota((PLANE, PLANE), 0), iota((PLANE, PLANE), 1)
    j, m = iota((LANES, LANES), 0), iota((LANES, LANES), 1)

    def ones(mask):
        return jnp.where(mask, 1.0, 0.0)

    def small(left, right):
        return jnp.dot(left.astype(BF16), right.astype(BF16), preferred_element_type=F32)

    def exact(left, right):
        return jnp.dot(left, right, precision=lax.Precision.HIGHEST, preferred_element_type=F32)

    same_y = (a >> 3) == (b >> 3)
    base = small(ones(same_y & (b < a)), counts)
    base = base + small(small(ones(same_y), counts), ones((j < Z) & (j < (m & (Z - 1)))))
    base = base + small(small(ones((b >> 3) < (a >> 3)), counts), ones(j < Z))
    count = jnp.sum(jnp.where(iota((PLANE, LANES), 1) < Z, counts, 0.0), axis=1, keepdims=True)
    count = jnp.sum(count, axis=0, keepdims=True)
    want = wrapped(picks[...], count)

    def standing(array):
        return jnp.concatenate([array, jnp.zeros((LANES - PLANE, LANES), F32)], axis=0).T[:Z]

    widen = ones((j == (m >> 1)) & (m < PLANE * DIRECT))
    rank = (iota((Z, LANES), 1) & (DIRECT - 1)).astype(F32)
    taken = rank < small(standing(counts), widen) - 0.5
    order = jnp.where(taken, exact(standing(base), widen) + rank, -1.0)
    taken = ones(taken)
    for z in range(Z):
        direct_pick[z, pl.ds(0, 2 * bound)] = ones(want == order[z : z + 1]).astype(BF16)
        direct_pick[z, pl.ds(2 * bound, 16)] = jnp.broadcast_to(taken[z : z + 1], (16, LANES)).astype(BF16)

    from_z = ones(j == ((m >> 1) & (Z - 1)))
    own_xc = (iota((PLANE, LANES), 0) & (XC - 1)) == (iota((PLANE, LANES), 1) >> 4)

    def folded(array):
        return jnp.sum(jnp.where(own_xc, array, 0.0).reshape(Y, XC, LANES), axis=1)

    rank = (iota((Y, LANES), 1) & (HOPPED - 1)).astype(F32) + DIRECT
    taken = rank < folded(small(counts, from_z)) - 0.5
    order = jnp.where(taken, folded(exact(base, from_z)) + rank, -1.0)
    taken = ones(taken)
    for y in range(Y):
        at = pl.ds(y * LANES, LANES)
        hop_pick[pl.ds(0, 2 * bound), at] = ones(want == order[y : y + 1]).astype(BF16)
        hop_pick[pl.ds(2 * bound, 16), at] = jnp.broadcast_to(taken[y : y + 1], (16, LANES)).astype(BF16)

    each = PLANE * DIRECT

    def settle(dz):
        awaited(me, in_buf, PLANE - 1 if dz == 0 else PLANE, send_sem, recv_sem.at[dz]).wait_recv()
        z = lax.rem(my_z + Z - dz, Z)
        for y in range(Y):
            direct[z, pl.ds(y * XC * DIRECT, XC * DIRECT)] = in_buf[pl.ds((y * Z + z) * XC, XC)].reshape(
                XC * DIRECT, width
            )
        return z

    for n, dz in enumerate(ORDER[:EARLY]):
        z = settle(dz)
        given = jnp.dot(direct_pick[z][:, :each], direct[z], preferred_element_type=F32)
        acc[...] = given if n == 0 else acc[...] + given
    awaited(me, in_hop, PLANE - 1, hop_send, hop_recv).wait_recv()
    hopped = in_hop[...].reshape(PLANE * Z * HOPPED, width)
    acc[...] += jnp.dot(hop_pick[...], hopped, preferred_element_type=F32)
    planes = [settle(dz) for dz in ORDER[EARLY:]]
    latest = jnp.concatenate([direct[z] for z in planes], axis=0)

    def gather(first, size):
        at = pl.ds(first, size)
        chosen = jnp.concatenate([direct_pick[z, at][:, :each] for z in planes], axis=1)
        return acc[at] + jnp.dot(chosen, latest, preferred_element_type=F32)

    half = bound // 2
    copies = []
    for part in range(4):
        rows_out = gather((1 - part % 2) * bound + part // 2 * half, half).astype(BF16)
        copies.append(exchange(me, part, rows_out, bound, outward, beside, side_send, side_recv))
    sums = gather(2 * bound, 16)[:1]

    lines = PLANE * CAP
    a, b = iota((lines, each), 0), iota((lines, each), 1)
    k = a & (CAP - 1)
    from_direct = ones((k < DIRECT) & (b == (a >> 2) * DIRECT + k)).astype(BF16)
    a, b = iota((lines, PLANE * Z * HOPPED), 0), iota((lines, PLANE * Z * HOPPED), 1)
    k = a & (CAP - 1)
    for z in range(Z):
        from_hop = ones((k >= DIRECT) & (b == (a >> 2) * (Z * HOPPED) + z * HOPPED + k - DIRECT)).astype(BF16)
        mixed = jnp.dot(from_direct, direct[z], preferred_element_type=F32)
        mixed = (mixed + jnp.dot(from_hop, hopped, preferred_element_type=F32)).astype(BF16)
        for y in range(Y):
            members[pl.ds((y * Z + z) * XC * CAP, XC * CAP)] = mixed[y * XC * CAP : (y + 1) * XC * CAP]
    heads, filled = filled_slots(members)
    close(me, members, filled, sums, copies, beside, best_ref, cent_ref)
    full_ref[...] = jnp.broadcast_to(jnp.max(heads, axis=1, keepdims=True), full_ref.shape)

    awaited(me, out_buf, DEVICES - 1, send_sem, recv_sem.at[0]).wait_send()
    awaited(me, out_spill, Z - 1, spill_send, spill_recv).wait_send()
    awaited(me, out_code, Z - 1, code_send, code_recv).wait_send()
    awaited(me, out_hop, PLANE - 1, hop_send, hop_recv).wait_send()
    awaited(me, out_count, PLANE - 1, count_send, count_recv).wait_send()


def per_device(embeddings, cluster_ids, boundary_slots):
    rows, width = embeddings.shape
    bound = boundary_slots.shape[2]
    labels, ranks = cluster_ids.reshape(1, rows), boundary_slots[0]
    line = jax.ShapeDtypeStruct((1, SLOTS), F32)
    vmem, anywhere = pl.BlockSpec(memory_space=pltpu.VMEM), pl.BlockSpec(memory_space=pl.ANY)
    dma = pltpu.SemaphoreType.DMA

    def buffers(per):
        return [
            pltpu.VMEM((rows, width), F32),
            pltpu.VMEM((1, rows), jnp.int32),
            pltpu.VMEM((2, bound), jnp.int32),
            pltpu.VMEM((rows, width), BF16),
            pltpu.VMEM((DEVICES, per, width), BF16),
            pltpu.VMEM((DEVICES, per, width), BF16),
            pltpu.VMEM((SLOTS, width), BF16),
            pltpu.VMEM((2 * bound, LANES), F32),
            pltpu.VMEM((2 * bound, width), BF16),
            pltpu.VMEM((2 * bound, width), BF16),
        ]

    sems = [dma((3,)), pltpu.SemaphoreType.REGULAR, dma, dma((Z,))]

    def call(body, outs, scratch, number):
        return pl.pallas_call(
            body,
            out_shape=outs,
            in_specs=[anywhere] * 3,
            out_specs=(vmem,) * len(outs),
            scratch_shapes=scratch,
            compiler_params=pltpu.CompilerParams(
                collective_id=number, has_side_effects=True, vmem_limit_bytes=48 << 20
            ),
        )(embeddings, labels, ranks)

    best, central, full = call(
        two_hop_kernel,
        (line, line, jax.ShapeDtypeStruct((1, LANES), F32)),
        buffers(DIRECT)
        + [
            pltpu.VMEM((Z, SPILL, width), BF16),
            pltpu.VMEM((Z, SPILL, width), BF16),
            pltpu.VMEM((Z, 8, LANES), BF16),
            pltpu.VMEM((Z, 8, LANES), BF16),
            pltpu.VMEM((PLANE, Z * HOPPED, width), BF16),
            pltpu.VMEM((PLANE, Z * HOPPED, width), BF16),
            pltpu.VMEM((PLANE, 8, LANES), BF16),
            pltpu.VMEM((PLANE, 8, LANES), BF16),
            pltpu.VMEM((Z, 2 * bound + 16, LANES), BF16),
            pltpu.VMEM((2 * bound + 16, PLANE * Z * HOPPED), BF16),
            pltpu.VMEM((2 * bound + 16, width), F32),
            pltpu.VMEM((Z, PLANE * DIRECT, width), BF16),
        ]
        + sems
        + [dma((3,)), dma((4,)), dma((4,))]
        + [dma] * 8,
        0,
    )

    def again():
        return tuple(call(four_slot_kernel, (line, line), buffers(CAP) + sems + [dma, dma((4,)), dma((4,))], 1))

    return lax.cond(full[0, 0] > 4.0, again, lambda: (best, central))


def solution(mesh):
    placed = (P(("dp", "rep"), None), P(("dp", "rep"), None), P(("dp", "rep"), None, None))
    return jax.shard_map(
        per_device,
        mesh=mesh,
        in_specs=placed,
        out_specs=(P(("dp", "rep"), None), P(("dp", "rep"), None)),
        check_vma=False,
    )
```

```python
import functools

import jax
import jax.numpy as jnp
from jax import lax
from jax.experimental import pallas as pl
from jax.experimental.pallas import tpu as pltpu
from jax.sharding import PartitionSpec as P

MESH = pl.DeviceIdType.MESH
SLOTS = 1024
CAP = 4
DIRECT = 2
HOPPED = CAP - DIRECT
SPILL = 16
Y, Z, X, C = 4, 8, 4, 2
XC = X * C
PLANE = Y * XC
DEVICES = Z * PLANE
SIDE = 16
LANES = 128
EPS = 1e-06
EMPTY = 2.0
FULL = 8.0
ORDER = (0, 1, 7, 2, 6, 4, 3, 5)
EARLY = 5
STRIDE = 13
F32 = jnp.float32
BF16 = jnp.bfloat16


def iota(shape, dim):
    return lax.broadcasted_iota(jnp.int32, shape, dim)


def rows_dot(a, b):
    return lax.dot_general(a, b, (((1,), (1,)), ((), ())), preferred_element_type=F32)


def device(flat):
    return (flat // C, lax.rem(flat, C))


def along_sublanes(row, size):
    turned = jnp.broadcast_to(row, (LANES, row.shape[1])).T
    return jnp.concatenate([turned] * (size // LANES), axis=1)


def earlier_equal(key, size):
    same = (along_sublanes(key, size) == key) & (iota((size, size), 0) < iota((size, size), 1))
    return jnp.sum(jnp.where(same, 1.0, 0.0), axis=0, keepdims=True)


def place():
    dp, core = lax.axis_index("dp"), lax.axis_index("rep")
    return dp * C + core, dp // (Z * X), lax.rem(dp // X, Z), lax.rem(dp, X), core


def row_mate(me, i):
    y, z, x, c = me // (Z * XC), lax.rem(me // XC, Z), lax.rem(me // C, X), lax.rem(me, C)
    return ((y * Z + lax.rem(z + i // C, Z)) * X + x) * C + lax.rem(c + i, C)


def column_mate(me, i):
    y, z, x, c = me // (Z * XC), lax.rem(me // XC, Z), lax.rem(me // C, X), lax.rem(me, C)
    return ((lax.rem(y + i // X, Y) * Z + z) * X + lax.rem(x + i, X)) * C + c


def greet(me):
    barrier = pltpu.get_barrier_semaphore()

    def one(i, _):
        pl.semaphore_signal(barrier, inc=1, device_id=device(row_mate(me, i)), device_id_type=MESH)
        pl.semaphore_signal(barrier, inc=1, device_id=device(column_mate(me, i)), device_id_type=MESH)
        return 0

    lax.fori_loop(1, SIDE, one, 0)


def pass_on(me, stage_sem):
    pl.semaphore_wait(pltpu.get_barrier_semaphore(), 2 * (SIDE - 1))

    def one(i, _):
        pl.semaphore_signal(stage_sem, inc=1, device_id=device(row_mate(me, i)), device_id_type=MESH)
        return 0

    lax.fori_loop(1, SIDE, one, 0)


def fetch(sources, targets, sems):
    copies = [pltpu.make_async_copy(s, t, sems.at[k]) for k, (s, t) in enumerate(zip(sources, targets))]
    for copy in copies:
        copy.start()
    return copies


def normalise(emb_ref, unit):
    rows = emb_ref.shape[0]
    step = 128

    def one(i, _):
        at = pl.ds(pl.multiple_of(i * step, step), step)
        emb = emb_ref[at, :]
        unit[at, :] = (emb * lax.rsqrt(jnp.sum(emb * emb, axis=1, keepdims=True) + EPS)).astype(BF16)
        return 0

    lax.fori_loop(0, rows // step, one, 0)


def build(target, unit, buf, total, per, full=None):
    rows, width = unit.shape
    step = 128

    def one(i, _):
        slot = (iota((step, rows), 0) + i * step).astype(F32)
        chosen = jnp.where(slot == target, 1.0, 0.0)
        some = jnp.sum(chosen, axis=1, keepdims=True)
        block = jnp.dot(chosen.astype(BF16), unit[...], preferred_element_type=F32)
        first = iota((step, width), 1) == 0
        block = jnp.where((some < 0.5) & first, EMPTY, block)
        if full is not None:
            block = jnp.where((full > 0.5) & first, FULL, block)
        buf[pl.ds(i * (step // per), step // per)] = block.astype(BF16).reshape(step // per, per, width)
        return 0

    lax.fori_loop(0, total // step, one, 0)


def turn_picks(bnd_ref, picks):
    bound = bnd_ref.shape[1]
    raw = bnd_ref[...].astype(F32)
    for side in range(2):
        picks[pl.ds(side * bound, bound)] = jnp.broadcast_to(raw[side : side + 1], (LANES, bound)).T


def in_plane(place_of_me, i):
    _, my_y, _, my_x, core = place_of_me
    i = lax.rem(i * STRIDE, PLANE)
    return lax.rem(my_y + i // XC, Y), lax.rem(my_x + i // C, X), lax.rem(core + i, C)


def send_one(place_of_me, dz, i, source, target, send_sem, recv_sem):
    y, x, c = in_plane(place_of_me, i)
    t = (y * Z + lax.rem(place_of_me[2] + dz, Z)) * X + x
    pltpu.make_async_remote_copy(
        source.at[t * C + c], target.at[place_of_me[0]], send_sem, recv_sem.at[dz],
        device_id=(t, c), device_id_type=MESH,
    ).start()


def send_group(place_of_me, dzs, source, target, send_sem, recv_sem, beside=None):
    def one(i, _):
        if beside is not None:
            beside(i)
        for dz in dzs:
            send_one(place_of_me, dz, i, source, target, send_sem, recv_sem)
        return 0

    for dz in dzs:
        if dz:
            send_one(place_of_me, dz, 0, source, target, send_sem, recv_sem)
    lax.fori_loop(1, PLANE, one, 0)


def awaited(me, ref, n, send_sem, recv_sem):
    view = ref.at[pl.ds(0, n)]
    return pltpu.make_async_remote_copy(
        view, view, send_sem, recv_sem, device_id=device(row_mate(me, 1)), device_id_type=MESH
    )


def exchange(me, part, rows, bound, outward, beside, side_send, side_recv):
    half = bound // 2
    side = 1 - part % 2
    at = pl.ds(side * bound + part // 2 * half, half)
    outward[at] = rows
    peer = lax.rem(me + 1, DEVICES) if side == 1 else lax.rem(me + DEVICES - 1, DEVICES)
    copy = pltpu.make_async_remote_copy(
        outward.at[at], beside.at[at], side_send.at[part], side_recv.at[part],
        device_id=device(peer), device_id_type=MESH,
    )
    copy.start()
    return copy, side, at


def filled_slots(members):
    corner = jnp.where(iota((8, LANES), 1) == 0, 1.0, 0.0).astype(BF16)
    heads = rows_dot(corner, members[:, :LANES])[:1]
    return heads, jnp.where(heads < 1.5, 1.0, 0.0)


def split_centre(sums, lines):
    direction = sums * lax.rsqrt(jnp.sum(sums * sums, axis=1, keepdims=True) + EPS)
    high = direction.astype(BF16)
    rest = direction - high.astype(F32)
    middle = rest.astype(BF16)
    low = (rest - middle.astype(F32)).astype(BF16)
    row = iota((lines, sums.shape[1]), 0)
    parts = jnp.where(row == 2, low.astype(F32), 0.0)
    parts = jnp.where(row == 1, middle.astype(F32), parts)
    return jnp.where(row == 0, high.astype(F32), parts).astype(BF16)


def close(me, members, filled, sums, copies, beside, best_ref, cent_ref):
    table = members[...]
    central = jnp.sum(rows_dot(split_centre(sums, 8), table), axis=0, keepdims=True)
    cent_ref[...] = jnp.where(filled > 0.5, central, 0.0)

    chunk = 256
    best = jnp.full((8, SLOTS), -1.0, F32)
    for first in range(0, SLOTS, chunk):
        scores = rows_dot(members[first : first + chunk], table)
        empty = members[first : first + chunk, :LANES][:, :1].astype(F32) > 1.5
        barred = empty | (iota((chunk, SLOTS), 0) + first == iota((chunk, SLOTS), 1))
        scores = jnp.where(barred, -1.0, scores)
        best = jnp.maximum(best, jnp.max(scores.reshape(chunk // 8, 8, SLOTS), axis=0))
    for copy, side, at in copies:
        copy.wait()
        scores = rows_dot(beside[at], table)
        top = jnp.max(scores.reshape(at.size // 8, 8, SLOTS), axis=0)
        there = me > 0 if side == 1 else me < DEVICES - 1
        best = jnp.maximum(best, jnp.where(there, top, -1.0))
    nearest = jnp.max(best, axis=0, keepdims=True)
    best_ref[...] = jnp.where(filled > 0.5, nearest, 0.0)


def wrapped(want, count):
    return want - jnp.floor((want + 0.5) / count) * count


def finish(me, members, picks, outward, beside, side_send, side_recv, best_ref, cent_ref):
    bound = outward.shape[0] // 2
    groups = SLOTS // LANES
    _, filled = filled_slots(members)
    stacked = jnp.concatenate([filled[:, k * LANES : (k + 1) * LANES] for k in range(groups)], axis=0)
    upto = jnp.where(iota((LANES, LANES), 0) <= iota((LANES, LANES), 1), 1.0, 0.0).astype(BF16)
    within = jnp.dot(stacked.astype(BF16), upto, preferred_element_type=F32)
    totals = jnp.sum(stacked, axis=1, keepdims=True)
    count = jnp.sum(totals, axis=0, keepdims=True)
    order = []
    before = jnp.zeros((1, 1), F32)
    for k in range(groups):
        order.append(jnp.where(stacked[k : k + 1] > 0.5, within[k : k + 1] + (before - 1.0), -1.0))
        before = before + totals[k : k + 1]
    table = members[...]
    copies = []
    half = bound // 2
    for part in range(4):
        want = wrapped(picks[pl.ds((1 - part % 2) * bound + part // 2 * half, half)], count)
        chosen = [jnp.where(want == order[k], 1.0, 0.0).astype(BF16) for k in range(groups)]
        rows = jnp.dot(jnp.concatenate(chosen, axis=1), table, preferred_element_type=F32).astype(BF16)
        copies.append(exchange(me, part, rows, bound, outward, beside, side_send, side_recv))
    weights = jnp.broadcast_to(filled, (8, SLOTS)).astype(BF16)
    sums = jnp.dot(weights, table, preferred_element_type=F32)[:1]
    close(me, members, filled, sums, copies, beside, best_ref, cent_ref)


def ranked(lab_ref):
    labels = lab_ref[...]
    rows = labels.shape[1]
    return labels, earlier_equal(labels.astype(F32), rows)


def four_slot_kernel(
    emb_hbm, lab_hbm, bnd_hbm, best_ref, cent_ref,
    emb_ref, lab_ref, bnd_ref, unit, out_buf, in_buf, members, picks, outward, beside,
    in_sem, stage_sem, send_sem, recv_sem, own_sem, side_send, side_recv,
):
    width = emb_ref.shape[1]
    here = place()
    me, _, my_z, _, _ = here
    got = fetch((emb_hbm, lab_hbm, bnd_hbm), (emb_ref, lab_ref, bnd_ref), in_sem)
    greet(me)
    for copy in got:
        copy.wait()
    labels, rank = ranked(lab_ref)
    normalise(emb_ref, unit)
    pass_on(me, stage_sem)
    build(labels.astype(F32) * CAP + rank, unit, out_buf, SLOTS, CAP)
    pl.semaphore_wait(stage_sem, SIDE - 1)
    own = pltpu.make_async_copy(out_buf.at[me], in_buf.at[me], own_sem)
    own.start()
    for dz in ORDER:
        send_group(here, (dz,), out_buf, in_buf, send_sem, recv_sem)
    turn_picks(bnd_ref, picks)
    own.wait()
    for dz in ORDER:
        awaited(me, in_buf, PLANE - 1 if dz == 0 else PLANE, send_sem, recv_sem.at[dz]).wait_recv()
        z = lax.rem(my_z + Z - dz, Z)
        for y in range(Y):
            first = (y * Z + z) * XC
            members[pl.ds(pl.multiple_of(first * CAP, XC * CAP), XC * CAP)] = in_buf[pl.ds(first, XC)].reshape(
                XC * CAP, width
            )
    finish(me, members, picks, outward, beside, side_send, side_recv, best_ref, cent_ref)
    awaited(me, out_buf, DEVICES - 1, send_sem, recv_sem.at[0]).wait_send()


def two_hop_kernel(
    emb_hbm, lab_hbm, bnd_hbm, best_ref, cent_ref, full_ref,
    emb_ref, lab_ref, bnd_ref, unit, out_buf, in_buf, turn, picks, outward, beside,
    out_spill, in_spill, out_code, in_code, out_hop, in_hop, out_count, in_count, direct_pick, hop_pick, acc, direct,
    in_sem, stage_sem, send_sem, recv_sem, own_sem, side_send, side_recv,
    spill_send, spill_recv, code_send, code_recv, hop_send, hop_recv, count_send, count_recv,
):
    rows, width = emb_ref.shape
    here = place()
    me, my_y, my_z, my_x, core = here
    mine = (my_y * X + my_x) * C + core
    got = fetch((emb_hbm, lab_hbm, bnd_hbm), (emb_ref, lab_ref, bnd_ref), in_sem)
    greet(me)
    got[1].wait()
    labels, rank = ranked(lab_ref)
    spilled = rank > DIRECT - 0.5
    plane = (labels >> 3) & (Z - 1)
    within = ((labels >> 6) << 3) | (labels & (XC - 1))
    key = jnp.where(spilled, plane, Z).astype(F32)
    spot = earlier_equal(key, rows)
    fits = spilled & (spot < SPILL - 0.5)
    full = jnp.max(jnp.where(spilled & (spot > SPILL - 0.5), 1.0, 0.0), axis=1, keepdims=True)
    direct_at = jnp.where(spilled, -1.0, labels.astype(F32) * DIRECT + rank)
    spill_at = jnp.where(fits, plane.astype(F32) * SPILL + spot, -1.0)
    code = within.astype(F32) * HOPPED + rank + (1 - DIRECT)
    got[0].wait()
    normalise(emb_ref, unit)

    lines = Z * SPILL
    chosen = jnp.where(iota((lines, rows), 0).astype(F32) == spill_at, 1.0, 0.0)
    out_spill[...] = (
        jnp.dot(chosen.astype(BF16), unit[...], preferred_element_type=F32).astype(BF16).reshape(Z, SPILL, width)
    )
    lane = iota((rows, LANES), 1).astype(F32)
    by_spot = jnp.where(along_sublanes(spot, LANES) == lane, 1.0, 0.0).astype(BF16)
    by_owner = jnp.where(along_sublanes(within.astype(F32), LANES) + PLANE == lane, 1.0, 0.0).astype(BF16)
    here_z = iota((Z, rows), 0) == plane
    coded = jnp.where(here_z & fits, code, 0.0).astype(BF16)
    counted = jnp.where(here_z, 1.0, 0.0).astype(BF16)
    info = jnp.dot(coded, by_spot, preferred_element_type=F32)
    info = info + jnp.dot(counted, by_owner, preferred_element_type=F32)
    out_code[...] = jnp.broadcast_to(info[:, None, :], (Z, 8, LANES)).astype(BF16)
    pass_on(me, stage_sem)

    def over(dz):
        z = lax.rem(my_z + dz, Z)
        to = ((my_y * Z + z) * X + my_x, core)
        pltpu.make_async_remote_copy(
            out_code.at[z], in_code.at[my_z], code_send, code_recv, device_id=to, device_id_type=MESH
        ).start()
        pltpu.make_async_remote_copy(
            out_spill.at[z], in_spill.at[my_z], spill_send, spill_recv, device_id=to, device_id_type=MESH
        ).start()

    for dz in (4, 3, 5, 2, 6, 1, 7):
        over(dz)
    build(direct_at, unit, out_buf, DEVICES * DIRECT, DIRECT, full)
    pl.semaphore_wait(stage_sem, SIDE - 1)
    own = fetch(
        (out_buf.at[me], out_spill.at[my_z], out_code.at[my_z]),
        (in_buf.at[me], in_spill.at[my_z], in_code.at[my_z]),
        own_sem,
    )
    send_group(here, ORDER[:EARLY], out_buf, in_buf, send_sem, recv_sem)
    got[2].wait()
    turn_picks(bnd_ref, picks)
    for copy in own:
        copy.wait()

    awaited(me, in_code, Z - 1, code_send, code_recv).wait_recv()
    awaited(me, in_spill, Z - 1, spill_send, spill_recv).wait_recv()
    info = jnp.max(in_code[...].astype(F32), axis=1)
    turned = jnp.concatenate([info] * (LANES // Z), axis=0).T[PLANE : 2 * PLANE]
    out_count[...] = jnp.broadcast_to(turned[:, None, :], (PLANE, 8, LANES)).astype(BF16)

    def tell(i, _):
        y, x, c = in_plane(here, i)
        pltpu.make_async_remote_copy(
            out_count.at[(y * X + x) * C + c], in_count.at[mine], count_send, count_recv,
            device_id=((y * Z + my_z) * X + x, c), device_id_type=MESH,
        ).start()
        return 0

    lax.fori_loop(1, PLANE, tell, 0)
    noted = pltpu.make_async_copy(out_count.at[mine], in_count.at[mine], own_sem.at[1])
    noted.start()
    spread = jnp.where(iota((LANES, LANES), 0) == (iota((LANES, LANES), 1) & (SPILL - 1)), 1.0, 0.0).astype(BF16)
    told = jnp.dot(info.astype(BF16), spread, preferred_element_type=F32)
    told = jnp.sum(jnp.where(iota((Z, LANES), 0) == (iota((Z, LANES), 1) >> 4), told, 0.0), axis=0, keepdims=True)
    owner = jnp.floor((told - 0.5) * (1.0 / HOPPED))
    line = owner * (Z * HOPPED) + (iota((1, lines), 1) >> 4).astype(F32) * HOPPED + (told - 1.0 - owner * HOPPED)
    line = jnp.where(told > 0.5, line, -1.0)
    came = in_spill[...].reshape(lines, width)
    step = 128
    for i in range(PLANE * Z * HOPPED // step):
        chosen = jnp.where((iota((step, lines), 0) + i * step).astype(F32) == line, 1.0, 0.0)
        some = jnp.sum(chosen, axis=1, keepdims=True)
        block = jnp.dot(chosen.astype(BF16), came, preferred_element_type=F32)
        block = jnp.where((some < 0.5) & (iota((step, width), 1) == 0), EMPTY, block)
        each = Z * HOPPED
        out_hop[pl.ds(i * (step // each), step // each)] = block.astype(BF16).reshape(step // each, each, width)

    def around(i):
        y, x, c = in_plane(here, i)
        pltpu.make_async_remote_copy(
            out_hop.at[(y * X + x) * C + c], in_hop.at[mine], hop_send, hop_recv,
            device_id=((y * Z + my_z) * X + x, c), device_id_type=MESH,
        ).start()

    kept = pltpu.make_async_copy(out_hop.at[mine], in_hop.at[mine], own_sem.at[0])
    kept.start()
    send_group(here, ORDER[EARLY:], out_buf, in_buf, send_sem, recv_sem, around)
    kept.wait()
    noted.wait()

    awaited(me, in_count, PLANE - 1, count_send, count_recv).wait_recv()
    bound = outward.shape[0] // 2
    counts = jnp.max(in_count[...].astype(F32), axis=1)
    a, b = iota((PLANE, PLANE), 0), iota((PLANE, PLANE), 1)
    j, m = iota((LANES, LANES), 0), iota((LANES, LANES), 1)

    def ones(mask):
        return jnp.where(mask, 1.0, 0.0)

    def small(left, right):
        return jnp.dot(left.astype(BF16), right.astype(BF16), preferred_element_type=F32)

    def exact(left, right):
        return jnp.dot(left, right, precision=lax.Precision.HIGHEST, preferred_element_type=F32)

    same_y = (a >> 3) == (b >> 3)
    base = small(ones(same_y & (b < a)), counts)
    base = base + small(small(ones(same_y), counts), ones((j < Z) & (j < (m & (Z - 1)))))
    base = base + small(small(ones((b >> 3) < (a >> 3)), counts), ones(j < Z))
    count = jnp.sum(jnp.where(iota((PLANE, LANES), 1) < Z, counts, 0.0), axis=1, keepdims=True)
    count = jnp.sum(count, axis=0, keepdims=True)
    want = wrapped(picks[...], count)

    def standing(array):
        return jnp.concatenate([array, jnp.zeros((LANES - PLANE, LANES), F32)], axis=0).T[:Z]

    widen = ones((j == (m >> 1)) & (m < PLANE * DIRECT))
    rank = (iota((Z, LANES), 1) & (DIRECT - 1)).astype(F32)
    taken = rank < small(standing(counts), widen) - 0.5
    order = jnp.where(taken, exact(standing(base), widen) + rank, -1.0)
    taken = ones(taken)
    for z in range(Z):
        direct_pick[z, pl.ds(0, 2 * bound)] = ones(want == order[z : z + 1]).astype(BF16)
        direct_pick[z, pl.ds(2 * bound, 16)] = jnp.broadcast_to(taken[z : z + 1], (16, LANES)).astype(BF16)

    from_z = ones(j == ((m >> 1) & (Z - 1)))
    own_xc = (iota((PLANE, LANES), 0) & (XC - 1)) == (iota((PLANE, LANES), 1) >> 4)

    def folded(array):
        return jnp.sum(jnp.where(own_xc, array, 0.0).reshape(Y, XC, LANES), axis=1)

    rank = (iota((Y, LANES), 1) & (HOPPED - 1)).astype(F32) + DIRECT
    taken = rank < folded(small(counts, from_z)) - 0.5
    order = jnp.where(taken, folded(exact(base, from_z)) + rank, -1.0)
    taken = ones(taken)
    for y in range(Y):
        at = pl.ds(y * LANES, LANES)
        hop_pick[pl.ds(0, 2 * bound), at] = ones(want == order[y : y + 1]).astype(BF16)
        hop_pick[pl.ds(2 * bound, 16), at] = jnp.broadcast_to(taken[y : y + 1], (16, LANES)).astype(BF16)

    each = PLANE * DIRECT
    step = 128
    for first in range(0, SLOTS, step):
        i = iota((step, 1), 0) + first
        if first < SLOTS // 2:
            z, y, xc, k = i >> 6, (i >> 4) & (Y - 1), (i >> 1) & (XC - 1), i & (DIRECT - 1)
        else:
            y, xc, z, k = (i >> 7) & (Y - 1), (i >> 4) & (XC - 1), (i >> 1) & (Z - 1), (i & (HOPPED - 1)) + DIRECT
        slot = ((y * Z + z) * XC + xc) * CAP + k
        turn[pl.ds(first, step)] = ones(slot == iota((step, SLOTS), 1)).astype(BF16)

    def settle(dz):
        awaited(me, in_buf, PLANE - 1 if dz == 0 else PLANE, send_sem, recv_sem.at[dz]).wait_recv()
        z = lax.rem(my_z + Z - dz, Z)
        for y in range(Y):
            direct[z, pl.ds(y * XC * DIRECT, XC * DIRECT)] = in_buf[pl.ds((y * Z + z) * XC, XC)].reshape(
                XC * DIRECT, width
            )
        return z

    for n, dz in enumerate(ORDER[:EARLY]):
        z = settle(dz)
        given = jnp.dot(direct_pick[z][:, :each], direct[z], preferred_element_type=F32)
        acc[...] = given if n == 0 else acc[...] + given
    awaited(me, in_hop, PLANE - 1, hop_send, hop_recv).wait_recv()
    hopped = in_hop[...].reshape(PLANE * Z * HOPPED, width)
    acc[...] += jnp.dot(hop_pick[...], hopped, preferred_element_type=F32)
    planes = [settle(dz) for dz in ORDER[EARLY:]]
    latest = jnp.concatenate([direct[z] for z in planes], axis=0)

    def gather(first, size):
        at = pl.ds(first, size)
        chosen = jnp.concatenate([direct_pick[z, at][:, :each] for z in planes], axis=1)
        return acc[at] + jnp.dot(chosen, latest, preferred_element_type=F32)

    half = bound // 2
    above, below = lax.rem(me + 1, DEVICES), lax.rem(me + DEVICES - 1, DEVICES)
    copies = []
    for part, (side, peer, skip, size) in enumerate(
        (
            (core, jnp.where(core == 1, above, below), 0, half),
            (core, jnp.where(core == 1, above, below), half, half),
            (1 - core, jnp.where(core == 1, below, above), 0, bound),
        )
    ):
        first = pl.multiple_of(side * bound + skip, half)
        outward[pl.ds(first, size)] = gather(first, size).astype(BF16)
        view = pl.ds(first, size)
        copy = pltpu.make_async_remote_copy(
            outward.at[view], beside.at[view], side_send.at[part], side_recv.at[part],
            device_id=device(peer), device_id_type=MESH,
        )
        copy.start()
        copies.append(copy)
    sums = gather(2 * bound, 16)[:1]

    part_size = SLOTS // 2
    tables = (direct[...].reshape(part_size, width), hopped)
    chunk = 512
    halves = []
    for own_table in tables:
        most = jnp.full((8, part_size), -1.0, F32)
        for table in tables:
            for first in range(0, part_size, chunk):
                cand = table[first : first + chunk]
                scores = rows_dot(cand, own_table)
                barred = cand[:, :LANES][:, :1].astype(F32) > 1.5
                if table is own_table:
                    barred = barred | (iota((chunk, part_size), 0) + first == iota((chunk, part_size), 1))
                scores = jnp.where(barred, -1.0, scores)
                most = jnp.maximum(most, jnp.max(scores.reshape(chunk // 8, 8, part_size), axis=0))
        halves.append(most)
    corner = jnp.where(iota((8, LANES), 1) == 0, 1.0, 0.0).astype(BF16)
    heads = jnp.concatenate([rows_dot(corner, table[:, :LANES])[:1] for table in tables], axis=1)
    centre = split_centre(sums, 16)
    central = []
    off_chip = (me > 0) & (me < DEVICES - 1)
    inner = pl.multiple_of(core * bound, bound)
    outer = pl.multiple_of((1 - core) * bound, bound)
    copies[2].wait()
    copies[0].wait()
    rows_in = jnp.concatenate([beside[pl.ds(inner, bound)], beside[pl.ds(outer, half)], centre], axis=0)
    for n, table in enumerate(tables):
        scores = rows_dot(rows_in, table)
        near = jnp.max(scores[:bound].reshape(bound // 8, 8, part_size), axis=0)
        far = jnp.max(scores[bound : bound + half].reshape(half // 8, 8, part_size), axis=0)
        halves[n] = jnp.maximum(halves[n], jnp.maximum(near, jnp.where(off_chip, far, -1.0)))
        central.append(jnp.sum(scores[bound + half : bound + half + 8], axis=0, keepdims=True))
    copies[1].wait()
    rows_in = beside[pl.ds(pl.multiple_of(outer + half, half), half)]
    for n, table in enumerate(tables):
        far = jnp.max(rows_dot(rows_in, table).reshape(half // 8, 8, part_size), axis=0)
        halves[n] = jnp.maximum(halves[n], jnp.where(off_chip, far, -1.0))
    nearest = jnp.max(jnp.concatenate(halves, axis=1), axis=0, keepdims=True)
    central = jnp.concatenate(central, axis=1)

    row = iota((8, SLOTS), 0)
    both = jnp.where(row < 4, nearest, central)
    both = jnp.where(heads < 1.5, both, 0.0)
    high = both.astype(BF16).astype(F32)
    middle = (both - high).astype(BF16).astype(F32)
    low = both - high - middle
    both = jnp.where((row & 3) == 0, high, jnp.where((row & 3) == 1, middle, jnp.where((row & 3) == 2, low, 0.0)))
    both = jnp.dot(both.astype(BF16), turn[...], preferred_element_type=F32)
    best_ref[...] = jnp.sum(both[:4], axis=0, keepdims=True)
    cent_ref[...] = jnp.sum(both[4:], axis=0, keepdims=True)
    full_ref[...] = jnp.broadcast_to(jnp.max(heads, axis=1, keepdims=True), full_ref.shape)

    awaited(me, out_buf, DEVICES - 1, send_sem, recv_sem.at[0]).wait_send()
    awaited(me, out_spill, Z - 1, spill_send, spill_recv).wait_send()
    awaited(me, out_code, Z - 1, code_send, code_recv).wait_send()
    awaited(me, out_hop, PLANE - 1, hop_send, hop_recv).wait_send()
    awaited(me, out_count, PLANE - 1, count_send, count_recv).wait_send()


def per_device(embeddings, cluster_ids, boundary_slots):
    rows, width = embeddings.shape
    bound = boundary_slots.shape[2]
    labels, ranks = cluster_ids.reshape(1, rows), boundary_slots[0]
    line = jax.ShapeDtypeStruct((1, SLOTS), F32)
    vmem, anywhere = pl.BlockSpec(memory_space=pltpu.VMEM), pl.BlockSpec(memory_space=pl.ANY)
    dma = pltpu.SemaphoreType.DMA

    def buffers(per):
        return [
            pltpu.VMEM((rows, width), F32),
            pltpu.VMEM((1, rows), jnp.int32),
            pltpu.VMEM((2, bound), jnp.int32),
            pltpu.VMEM((rows, width), BF16),
            pltpu.VMEM((DEVICES, per, width), BF16),
            pltpu.VMEM((DEVICES, per, width), BF16),
            pltpu.VMEM((SLOTS, width), BF16),
            pltpu.VMEM((2 * bound, LANES), F32),
            pltpu.VMEM((2 * bound, width), BF16),
            pltpu.VMEM((2 * bound, width), BF16),
        ]

    sems = [dma((3,)), pltpu.SemaphoreType.REGULAR, dma, dma((Z,))]

    def call(body, outs, scratch, number):
        return pl.pallas_call(
            body,
            out_shape=outs,
            in_specs=[anywhere] * 3,
            out_specs=(vmem,) * len(outs),
            scratch_shapes=scratch,
            compiler_params=pltpu.CompilerParams(
                collective_id=number, has_side_effects=True, vmem_limit_bytes=48 << 20
            ),
        )(embeddings, labels, ranks)

    best, central, full = call(
        two_hop_kernel,
        (line, line, jax.ShapeDtypeStruct((1, LANES), F32)),
        buffers(DIRECT)
        + [
            pltpu.VMEM((Z, SPILL, width), BF16),
            pltpu.VMEM((Z, SPILL, width), BF16),
            pltpu.VMEM((Z, 8, LANES), BF16),
            pltpu.VMEM((Z, 8, LANES), BF16),
            pltpu.VMEM((PLANE, Z * HOPPED, width), BF16),
            pltpu.VMEM((PLANE, Z * HOPPED, width), BF16),
            pltpu.VMEM((PLANE, 8, LANES), BF16),
            pltpu.VMEM((PLANE, 8, LANES), BF16),
            pltpu.VMEM((Z, 2 * bound + 16, LANES), BF16),
            pltpu.VMEM((2 * bound + 16, PLANE * Z * HOPPED), BF16),
            pltpu.VMEM((2 * bound + 16, width), F32),
            pltpu.VMEM((Z, PLANE * DIRECT, width), BF16),
        ]
        + sems
        + [dma((3,)), dma((4,)), dma((4,))]
        + [dma] * 8,
        0,
    )

    def again():
        return tuple(call(four_slot_kernel, (line, line), buffers(CAP) + sems + [dma, dma((4,)), dma((4,))], 1))

    return lax.cond(full[0, 0] > 4.0, again, lambda: (best, central))


def solution(mesh):
    placed = (P(("dp", "rep"), None), P(("dp", "rep"), None), P(("dp", "rep"), None, None))
    return jax.shard_map(
        per_device,
        mesh=mesh,
        in_specs=placed,
        out_specs=(P(("dp", "rep"), None), P(("dp", "rep"), None)),
        check_vma=False,
    )
```
